32 devices in a mesh: row: 8 (over y, x, core), col: 4 (over z).
Axes of the slice: x: 2, y: 2, z: 4, core: 2. Of those that a mesh axis runs over, the one named last changes fastest.
Arguments:
- col_samples: float32 [16, 2, 2048, 128], P('row', None, 'col'), may hold values from -6 to 6
- row_samples: float32 [16, 2, 128, 2048], P('row', None, None, 'col'), may hold values from -6 to 6
- pivot_rows: int32 [16, 128], P('row'), may hold values from 0 to 2047
- rank_blocks: int32 [16], P('row'), may hold values from 1 to 8
- upper_inverse: float32 [2, 2048, 2048], P(None, 'col', 'row'), as said below
- upanel_left: float32 [4, 2, 2048, 128], P('col'), may hold values from -0.125 to 0.125
Outputs:
- panel_right: float32 [16, 2, 128, 2048], P('row', None, None, 'col')
- cores: float32 [16, 4, 2, 128, 128], P('row', 'col')
The draws below stay inside these ranges and needn't reach their ends.
Inputs may be any that keep to these rules, and one draw needn't show every extreme that they name: `rank_blocks`: the tile's rank is 16 times this. `upper_inverse`: zero below the diagonal in both parts.
All inputs are finite; a program needn't handle non-finite values.
Results may differ from the reference program's by a relative error of at most 0.00007.
Values sent between devices are 32-bit elements; how exact they have to be, the bound alone decides.
A program may use at most 64 MiB of HBM per device.

```python
import jax
import jax.numpy as jnp
from jax import lax

B = 2048
R = 128
RANK_STEP = 16
NT = 16
NJ = 4


def draw_upper_inverse(key, part):
    first_key, second_key = jax.random.split(key)
    base = jax.random.normal(first_key, (2, B, B), jnp.float32)
    rows_index = lax.broadcasted_iota(jnp.int32, (2, B, B), 1)
    cols_index = lax.broadcasted_iota(jnp.int32, (2, B, B), 2)
    component = lax.broadcasted_iota(jnp.int32, (2, B, B), 0)
    upper = jnp.where(cols_index >= rows_index, base * (1.0 / B ** 0.5), 0.0)
    diagonal = jax.random.uniform(second_key, (2, B, B), jnp.float32, 0.5, 1.5)
    on_diagonal = (cols_index == rows_index) & (component == 0)
    return upper + jnp.where(on_diagonal, diagonal, 0.0)


def plant(drawn, rng, low, top_value):
    dims = drawn.shape
    spot = [jax.random.randint(jax.random.fold_in(rng, axis), (), 0, dims[axis]) for axis in range(len(dims))]
    drawn = drawn.at[tuple(spot)].set(low)
    longest = dims.index(max(dims))
    spot[longest] = (spot[longest] + 1) % dims[longest]
    return drawn.at[tuple(spot)].set(top_value)


def block_levels(rng, shape, cuts, least, largest):
    gain = 1.0
    for position, blocks in cuts:
        heights = jax.random.uniform(jax.random.fold_in(jax.random.fold_in(rng, 6), position), (blocks,), jnp.float32, least / len(cuts), largest / len(cuts))
        gain = gain * jnp.repeat(jnp.exp(heights), shape[position] // blocks).reshape((-1,) + (1,) * (len(shape) - 1 - position))
    return gain


def normal_values(rng, dims, deviation, limit, shards=(), kind=jnp.bfloat16):
    values = deviation * jax.random.normal(rng, dims, jnp.float32)
    if shards:
        values = values * block_levels(rng, dims, shards, -0.22, 0.18)
    return jnp.clip(values, -limit, limit).astype(kind)


def setup_inputs(seed: int = 0) -> dict:
    streams_of = jax.random.split(jax.random.key(seed), 7)
    col_samples = normal_values(streams_of[0], (NT, 2, B, R), 1.0, 6.0, ((0, 8), (2, 4)), jnp.float32)
    row_samples = normal_values(streams_of[1], (NT, 2, R, B), 1.0, 6.0, ((0, 8), (3, 4)), jnp.float32)
    pivot_rows = plant(jax.random.randint(streams_of[2], (NT, R), 0, B), jax.random.fold_in(streams_of[2], 1), 0, B - 1).astype(jnp.int32)
    rank_blocks = plant(jax.random.randint(streams_of[3], (NT,), 1, R // RANK_STEP + 1), jax.random.fold_in(streams_of[3], 1), 1, (R // RANK_STEP + 1) - 1).astype(jnp.int32)
    upper_inverse = draw_upper_inverse(jax.random.fold_in(streams_of[6], 71), 0)
    upanel_left = normal_values(streams_of[5], (NJ, 2, B, R), B ** -0.5, 0.125, ((0, 4),), jnp.float32)
    return {"col_samples": col_samples, "row_samples": row_samples, "pivot_rows": pivot_rows, "rank_blocks": rank_blocks, "upper_inverse": upper_inverse, "upanel_left": upanel_left}


def complex_product(pattern, left_real, left_imag, right_real, right_imag):
    def single(left, right):
        return jnp.einsum(pattern, left, right, precision=lax.Precision.HIGHEST, preferred_element_type=jnp.float32)
    real_part = single(left_real, right_real) - single(left_imag, right_imag)
    imag_part = single(left_real, right_imag) + single(left_imag, right_real)
    return real_part, imag_part


def scale_rows(values, weight_real, weight_imag):
    wr = weight_real[:, :, None]
    wi = weight_imag[:, :, None]
    real_part = values[:, 0] * wr - values[:, 1] * wi
    imag_part = values[:, 0] * wi + values[:, 1] * wr
    return jnp.stack((real_part, imag_part), axis=1)


def reference(col_samples, row_samples, pivot_rows, rank_blocks, upper_inverse, upanel_left):
    count = col_samples.shape[0]
    index = jnp.broadcast_to(pivot_rows[:, None, None, :], (count, 2, 1, R)).astype(jnp.int32)
    entries = jnp.take_along_axis(col_samples, index, axis=2)[:, :, 0, :]
    levels = lax.broadcasted_iota(jnp.int32, (1, R), 1)
    keeping = (levels < RANK_STEP * rank_blocks[:, None]).astype(jnp.float32)
    magnitude = jnp.maximum(entries[:, 0] * entries[:, 0] + entries[:, 1] * entries[:, 1], 1.0)
    factor_real = keeping * entries[:, 0] / magnitude
    factor_imag = -keeping * entries[:, 1] / magnitude
    scaled = scale_rows(row_samples, factor_real, factor_imag)
    real_part, imag_part = complex_product("trk,kn->trn", scaled[:, 0], scaled[:, 1], upper_inverse[0], upper_inverse[1])
    panel_right = jnp.stack((real_part, imag_part), axis=1)
    core_real, core_imag = complex_product("trn,jns->tjrs", panel_right[:, 0], panel_right[:, 1], upanel_left[:, 0], upanel_left[:, 1])
    cores = jnp.stack((core_real, core_imag), axis=2)
    return panel_right, cores
```

```python
import functools
import math

import jax
import jax.numpy as jnp
from jax import lax
from jax.experimental import pallas as pl
from jax.experimental.pallas import tpu as pltpu
from jax.sharding import PartitionSpec as P

RANK_STEP = 16
MESH = pl.DeviceIdType.MESH


def split(x):
    high = x.astype(jnp.bfloat16)
    low = (x - high.astype(jnp.float32)).astype(jnp.bfloat16)
    return high, low


def dot3(xh, xl, uh, ul):
    def single(a, b):
        return jnp.dot(a, b, preferred_element_type=jnp.float32)

    return single(xh, uh) + (single(xh, ul) + single(xl, uh))


def kernel(
    n_rows, n_cols,
    row_ref, u_ref, up_ref, col_ref, piv_ref, rank_ref,
    panel_ref, cores_ref,
    xh, xl, us, ps, pr, fin, lz, lg, ks, kr, eb,
    u_loc, u_send, u_sib, u_fwd, u_recv,
    p_send, p_recv,
    lz_loc, lz_send, lz_recv, lg_loc, lg_send, lg_sib, lg_fwd, lg_recv,
    k_send, k_recv, e_send, e_recv,
):
    r, c = lax.axis_index("row"), lax.axis_index("col")
    chips = n_rows // 2
    nx = math.isqrt(chips)
    ny = chips // nx
    q, h = r // 2, r % 2
    qy, qx = q // nx, q % nx
    tiles, _, ranks, wc = row_ref.shape
    nsub, sw = us.shape[1], us.shape[4]
    wq = lz.shape[1]
    half = tiles * ranks
    sib = (q * 2 + 1 - h, c)

    def ahead(d):
        return ((qy + d // nx) % ny) * nx + (qx + d % nx) % nx

    def behind(d):
        return ((qy + ny - d // nx) % ny) * nx + (qx + nx - d % nx) % nx

    def rcopy(src, dst, ssem, rsem, dev):
        return pltpu.make_async_remote_copy(
            src_ref=src, dst_ref=dst, send_sem=ssem, recv_sem=rsem, device_id=dev, device_id_type=MESH
        )

    def u_out(d, s):
        return rcopy(
            u_ref.at[:, :, s * sw:(s + 1) * sw], us.at[r, s], u_send.at[d, s], u_recv.at[r, s],
            (behind(d) * 2 + h, c),
        )

    def u_side(s):
        return rcopy(u_ref.at[:, :, s * sw:(s + 1) * sw], us.at[r, s], u_sib.at[s], u_recv.at[r, s], sib)

    def u_forward(d, s, b):
        return rcopy(us.at[b, s], us.at[b, s], u_fwd.at[d, s], u_recv.at[b, s], sib)

    def p_up(b, s):
        return rcopy(ps.at[b, s], pr.at[b, s], p_send.at[b, s], p_recv.at[b, s], (r, c + 1))

    def lz_out(k):
        to = (c + k) % n_cols
        start = pl.multiple_of(to * wc + q * wq, wq)
        return rcopy(up_ref.at[0, h, pl.ds(start, wq), :], lz.at[c], lz_send.at[k], lz_recv.at[c], (r, to))

    def lg_out(d):
        return rcopy(lz, lg.at[h, q], lg_send.at[d], lg_recv.at[h, q], (behind(d) * 2 + h, c))

    def lg_side():
        return rcopy(lz, lg.at[h, q], lg_sib.at[0], lg_recv.at[h, q], sib)

    def lg_forward(d):
        b = ahead(d)
        return rcopy(lg.at[h, b], lg.at[h, b], lg_fwd.at[d], lg_recv.at[h, b], sib)

    def k_out(k):
        to = (c + k) % n_cols
        return rcopy(ks.at[k], kr.at[c], k_send.at[k], k_recv.at[c], (r, to))

    def e_out(k):
        return rcopy(eb.at[c], eb.at[c], e_send.at[k], e_recv.at[c], (r, (c + k) % n_cols))

    def each(first, last, body):
        lax.fori_loop(first, last, lambda i, z: (body(i), z)[1], 0)

    own = [
        pltpu.make_async_copy(u_ref.at[:, :, s * sw:(s + 1) * sw], us.at[r, s], u_loc.at[s]) for s in range(nsub)
    ]
    for copy in own:
        copy.start()
    mine = pl.multiple_of(c * wc + q * wq, wq)
    lz_own = pltpu.make_async_copy(up_ref.at[0, h, pl.ds(mine, wq), :], lz.at[c], lz_loc.at[0])
    lz_own.start()
    barrier = pltpu.get_barrier_semaphore()

    def signal(dev):
        pl.semaphore_signal(barrier, inc=1, device_id=dev, device_id_type=MESH)

    signal(sib)
    each(1, chips, lambda d: signal((behind(d) * 2 + h, c)))
    each(1, n_cols, lambda k: signal((r, (c + k) % n_cols)))
    pl.semaphore_wait(barrier, 1 + (chips - 1) + (n_cols - 1))

    early = min(3, chips)

    @pl.when(q >= c)
    def _():
        for s in range(nsub):
            u_side(s).start()

        def send(d):
            for s in range(nsub):
                u_out(d, s).start()

        each(1, early, send)

    each(1, n_cols, lambda k: lz_out(k).start())

    for i in range(tiles):
        for p in range(2):
            a, b = split(row_ref[i, p])
            at = pl.ds(p * half + i * ranks, ranks)
            xh[at, :] = a
            xl[at, :] = b

    pos = c * wc + lax.broadcasted_iota(jnp.int32, (wc, ranks), 0)
    parts = []
    for i in range(tiles):
        hit = pos == piv_ref[i:i + 1, :]
        for p in range(2):
            parts.append(jnp.sum(jnp.where(hit, col_ref[i, p], 0.0), axis=0, keepdims=True))
    parts.append(jnp.zeros((eb.shape[1] - 2 * tiles, ranks), jnp.float32))
    eb[c] = jnp.concatenate(parts, axis=0)
    each(1, n_cols, lambda k: e_out(k).start())
    for copy in own:
        copy.wait()

    total = chips * nsub * 2

    def unit(u, carry):
        d, s, e = u // (2 * nsub), (u // 2) % nsub, u % 2
        t = ahead(d)
        b = t * 2 + (h + e) % 2

        @pl.when(u == 2 * nsub)
        def _():
            lz_own.wait()
            each(1, n_cols, lambda k: rcopy(
                lz.at[(c + k) % n_cols], lz.at[(c + k) % n_cols], lz_send.at[k], lz_recv.at[(c + k) % n_cols], sib
            ).wait_recv())
            lg_side().start()
            pltpu.make_async_copy(lz, lg.at[h, q], lg_loc.at[0]).start()
            each(1, chips, lambda d2: lg_out(d2).start())

            @pl.when(q >= c)
            def _():
                def send(d2):
                    for s2 in range(nsub):
                        u_out(d2, s2).start()

                each(early, chips, send)

        @pl.when(u == total - 2 * nsub)
        def _():
            def pass_on(d2):
                o = ahead(d2)
                rcopy(lz, lg.at[h, o], lg_send.at[d2], lg_recv.at[h, o], sib).wait_recv()
                lg_forward(d2).start()

            each(1, chips, pass_on)

        @pl.when(t >= c)
        def _():
            @pl.when(jnp.logical_or(d > 0, e > 0))
            def _():
                rcopy(us.at[b, s], us.at[b, s], u_fwd.at[d, s], u_recv.at[b, s], sib).wait_recv()

            @pl.when(jnp.logical_and(d > 0, e == 0))
            def _():
                u_forward(d, s, b).start()

            ur, ui = us[b, s, 0], us[b, s, 1]
            uh, ul = split(jnp.concatenate([ur, ui], axis=1))
            prod = dot3(xh[...], xl[...], uh, ul)
            fin[0:half] = prod[:half, :sw] - prod[half:, sw:]
            fin[half:2 * half] = prod[:half, sw:] + prod[half:, :sw]

            @pl.when(c > 0)
            def _():
                rcopy(ps.at[b, s], pr.at[b, s], p_send.at[b, s], p_recv.at[b, s], sib).wait_recv()
                ps[b, s] = fin[...] + pr[b, s]

            @pl.when(c == 0)
            def _():
                ps[b, s] = fin[...]

            @pl.when(t > c)
            def _():
                p_up(b, s).start()

        return carry

    lax.fori_loop(0, total, unit, 0)

    each(1, n_cols, lambda k: rcopy(
        eb.at[(c + k) % n_cols], eb.at[(c + k) % n_cols], e_send.at[k], e_recv.at[(c + k) % n_cols], sib
    ).wait_recv())
    entries = jnp.sum(eb[...], axis=0)
    lines = []
    levels = lax.broadcasted_iota(jnp.int32, (1, ranks), 1)
    for i in range(tiles):
        er, ei = entries[2 * i:2 * i + 1], entries[2 * i + 1:2 * i + 2]
        keep = (levels < RANK_STEP * rank_ref[i]).astype(jnp.float32)
        mag = jnp.maximum(er * er + ei * ei, 1.0)
        lines.append(keep * er / mag)
        lines.append(-keep * ei / mag)
    lines.append(jnp.zeros((128 - 2 * tiles, ranks), jnp.float32))
    turned = jnp.concatenate(lines, axis=0).T
    for i in range(tiles):
        fr, fi = turned[:, 2 * i:2 * i + 1], turned[:, 2 * i + 1:2 * i + 2]
        lr, li = i * ranks, half + i * ranks
        vr, vi = [], []
        for hh in range(2):
            for s in range(nsub):
                vr.append(ps[2 * c + hh, s, lr:lr + ranks, :])
                vi.append(ps[2 * c + hh, s, li:li + ranks, :])
        vr, vi = jnp.concatenate(vr, axis=1), jnp.concatenate(vi, axis=1)
        wr = vr * fr - vi * fi
        wi = vr * fi + vi * fr
        panel_ref[i, 0] = wr
        panel_ref[i, 1] = wi
        a, b = split(wr)
        xh[lr:lr + ranks, :] = a
        xl[lr:lr + ranks, :] = b
        a, b = split(wi)
        xh[li:li + ranks, :] = a
        xl[li:li + ranks, :] = b

    pltpu.make_async_copy(lz, lg.at[h, q], lg_loc.at[0]).wait()
    each(0, chips, lambda o: rcopy(
        lz, lg.at[1 - h, o], lg_sib.at[0], lg_recv.at[1 - h, o], sib
    ).wait_recv())

    def core(k0, carry):
        k = (k0 + 1) % n_cols
        j = (c + k) % n_cols
        lr = lg[0, :, j].reshape(wc, lz.shape[2])
        li = lg[1, :, j].reshape(wc, lz.shape[2])
        rank2 = lz.shape[2]
        uh, ul = split(jnp.concatenate([lr, li], axis=1))
        prod = dot3(xh[...], xl[...], uh, ul)
        real = prod[:half, :rank2] - prod[half:, rank2:]
        imag = prod[:half, rank2:] + prod[half:, :rank2]
        for i in range(tiles):
            ks[k, i, 0] = real[i * ranks:(i + 1) * ranks]
            ks[k, i, 1] = imag[i * ranks:(i + 1) * ranks]

        @pl.when(k > 0)
        def _():
            k_out(k).start()

        return carry

    lax.fori_loop(0, n_cols, core, 0)
    cores_ref[:, 0] = ks[0]

    def gather(k):
        o = (c + k) % n_cols
        rcopy(ks.at[k], kr.at[o], k_send.at[k], k_recv.at[o], sib).wait_recv()
        cores_ref[:, 0] = cores_ref[:, 0] + kr[o]

    each(1, n_cols, gather)

    @pl.when(q >= c)
    def _():
        for s in range(nsub):
            u_side(s).wait_send()

        def left(d):
            for s in range(nsub):
                u_out(d, s).wait_send()

        each(1, chips, left)

    def rest(d):
        t = ahead(d)

        @pl.when(jnp.logical_and(t >= c, d > 0))
        def _():
            for s in range(nsub):
                u_forward(d, s, t * 2 + h).wait_send()

        @pl.when(t > c)
        def _():
            for s in range(nsub):
                for e in range(2):
                    p_up(t * 2 + e, s).wait_send()

        @pl.when(d > 0)
        def _():
            lg_out(d).wait_send()
            lg_forward(d).wait_send()

    each(0, chips, rest)
    lg_side().wait_send()

    def tail(k):
        lz_out(k).wait_send()
        k_out(k).wait_send()
        e_out(k).wait_send()

    each(1, n_cols, tail)


def on_device(n_rows, n_cols, col_samples, row_samples, pivot_rows, rank_blocks, upper_inverse, upanel_left):
    tiles, _, ranks, wc = row_samples.shape
    wr = upper_inverse.shape[2]
    left_ranks = upanel_left.shape[3]
    chips = n_rows // 2
    if chips != n_cols or wc != 2 * wr:
        raise ValueError("unsupported mesh")
    nsub = max(wr // 128, 1)
    sw = wr // nsub
    wq = wc // chips
    m = 2 * tiles * ranks
    f32, bf16 = jnp.float32, jnp.bfloat16
    dma = pltpu.SemaphoreType.DMA
    vmem = pl.BlockSpec(memory_space=pltpu.VMEM)
    hbm = pl.BlockSpec(memory_space=pl.ANY)
    return pl.pallas_call(
        functools.partial(kernel, n_rows, n_cols),
        out_shape=(
            jax.ShapeDtypeStruct((tiles, 2, ranks, wc), f32),
            jax.ShapeDtypeStruct((tiles, 1, 2, ranks, left_ranks), f32),
        ),
        in_specs=[vmem, hbm, hbm, vmem, vmem, pl.BlockSpec(memory_space=pltpu.SMEM)],
        out_specs=(vmem, vmem),
        scratch_shapes=[
            pltpu.VMEM((m, wc), bf16),
            pltpu.VMEM((m, wc), bf16),
            pltpu.VMEM((n_rows, nsub, 2, wc, sw), f32),
            pltpu.VMEM((n_rows, nsub, m, sw), f32),
            pltpu.VMEM((n_rows, nsub, m, sw), f32),
            pltpu.VMEM((m, sw), f32),
            pltpu.VMEM((n_cols, wq, left_ranks), f32),
            pltpu.VMEM((2, chips, n_cols, wq, left_ranks), f32),
            pltpu.VMEM((n_cols, tiles, 2, ranks, left_ranks), f32),
            pltpu.VMEM((n_cols, tiles, 2, ranks, left_ranks), f32),
            pltpu.VMEM((n_cols, -(-2 * tiles // 8) * 8, ranks), f32),
            dma((nsub,)), dma((chips, nsub)), dma((nsub,)), dma((chips, nsub)), dma((n_rows, nsub)),
            dma((n_rows, nsub)), dma((n_rows, nsub)),
            dma((1,)), dma((n_cols,)), dma((n_cols,)), dma((1,)), dma((chips,)), dma((1,)), dma((chips,)),
            dma((2, chips)),
            dma((n_cols,)), dma((n_cols,)), dma((n_cols,)), dma((n_cols,)),
        ],
        compiler_params=pltpu.CompilerParams(
            collective_id=0, has_side_effects=True, vmem_limit_bytes=56 * 1024 * 1024
        ),
    )(row_samples, upper_inverse, upanel_left, col_samples, pivot_rows, rank_blocks)


def solution(mesh):
    in_specs = (
        P("row", None, "col", None),
        P("row", None, None, "col"),
        P("row", None),
        P("row"),
        P(None, "col", "row"),
        P("col", None, None, None),
    )
    out_specs = (P("row", None, None, "col"), P("row", "col", None, None, None))
    body = functools.partial(on_device, mesh.shape["row"], mesh.shape["col"])
    return jax.shard_map(body, mesh=mesh, in_specs=in_specs, out_specs=out_specs, check_vma=False)
```

```python
import functools
import math

import jax
import jax.numpy as jnp
from jax import lax
from jax.experimental import pallas as pl
from jax.experimental.pallas import tpu as pltpu
from jax.sharding import PartitionSpec as P

RANK_STEP = 16
MESH = pl.DeviceIdType.MESH


def split(x):
    high = x.astype(jnp.bfloat16)
    low = (x - high.astype(jnp.float32)).astype(jnp.bfloat16)
    return high, low


def dot3(xh, xl, uh, ul):
    def single(a, b):
        return jnp.dot(a, b, preferred_element_type=jnp.float32)

    return single(xh, uh) + (single(xh, ul) + single(xl, uh))


def kernel(
    n_rows, n_cols,
    row_ref, u_ref, up_ref, col_ref, piv_ref, rank_ref,
    panel_ref, cores_ref,
    xh, xl, ch, cl, us, ps, pr, fin, lz, lg, ks, kr, eb,
    u_loc, u_send, u_sib, u_fwd, u_recv,
    p_send, p_recv,
    lz_loc, lz_send, lz_recv, lg_loc, lg_send, lg_sib, lg_fwd, lg_recv,
    k_send, k_recv, e_send, e_recv,
):
    r, c = lax.axis_index("row"), lax.axis_index("col")
    chips = n_rows // 2
    nx = math.isqrt(chips)
    ny = chips // nx
    q, h = r // 2, r % 2
    qy, qx = q // nx, q % nx
    tiles, _, ranks, wc = row_ref.shape
    nsub, sw = us.shape[1], us.shape[4]
    wq = lz.shape[1]
    half = tiles * ranks
    sib = (q * 2 + 1 - h, c)

    def ahead(d):
        return ((qy + d // nx) % ny) * nx + (qx + d % nx) % nx

    def behind(d):
        return ((qy + ny - d // nx) % ny) * nx + (qx + nx - d % nx) % nx

    def rcopy(src, dst, ssem, rsem, dev):
        return pltpu.make_async_remote_copy(
            src_ref=src, dst_ref=dst, send_sem=ssem, recv_sem=rsem, device_id=dev, device_id_type=MESH
        )

    def u_out(d, s):
        return rcopy(
            u_ref.at[:, :, s * sw:(s + 1) * sw], us.at[r, s], u_send.at[d, s], u_recv.at[r, s],
            (behind(d) * 2 + h, c),
        )

    def u_side(s):
        return rcopy(u_ref.at[:, :, s * sw:(s + 1) * sw], us.at[r, s], u_sib.at[s], u_recv.at[r, s], sib)

    def u_forward(t, s, b):
        return rcopy(us.at[b, s], us.at[b, s], u_fwd.at[t, s], u_recv.at[b, s], sib)

    def p_up(b, s):
        return rcopy(ps.at[b, s], pr.at[b, s], p_send.at[b, s], p_recv.at[b, s], (r, c + 1))

    def lz_out(k):
        to = (c + k) % n_cols
        start = pl.multiple_of(to * wc + q * wq, wq)
        return rcopy(up_ref.at[0, h, pl.ds(start, wq), :], lz.at[c], lz_send.at[k], lz_recv.at[c], (r, to))

    def lg_out(d):
        return rcopy(lz, lg.at[h, q], lg_send.at[d], lg_recv.at[h, q], (behind(d) * 2 + h, c))

    def lg_side():
        return rcopy(lz, lg.at[h, q], lg_sib.at[0], lg_recv.at[h, q], sib)

    def lg_forward(d):
        b = ahead(d)
        return rcopy(lg.at[h, b], lg.at[h, b], lg_fwd.at[d], lg_recv.at[h, b], sib)

    def k_out(k):
        to = (c + k) % n_cols
        return rcopy(ks.at[k], kr.at[c], k_send.at[k], k_recv.at[c], (r, to))

    def e_out(k):
        return rcopy(eb.at[c], eb.at[c], e_send.at[k], e_recv.at[c], (r, (c + k) % n_cols))

    def each(first, last, body):
        lax.fori_loop(first, last, lambda i, z: (body(i), z)[1], 0)

    own = [
        pltpu.make_async_copy(u_ref.at[:, :, s * sw:(s + 1) * sw], us.at[r, s], u_loc.at[s]) for s in range(nsub)
    ]
    for copy in own:
        copy.start()
    mine = pl.multiple_of(c * wc + q * wq, wq)
    lz_own = pltpu.make_async_copy(up_ref.at[0, h, pl.ds(mine, wq), :], lz.at[c], lz_loc.at[0])
    lz_own.start()
    barrier = pltpu.get_barrier_semaphore()

    def signal(dev):
        pl.semaphore_signal(barrier, inc=1, device_id=dev, device_id_type=MESH)

    signal(sib)
    each(1, chips, lambda d: signal((behind(d) * 2 + h, c)))
    each(1, n_cols, lambda k: signal((r, (c + k) % n_cols)))
    pl.semaphore_wait(barrier, 1 + (chips - 1) + (n_cols - 1))

    early = min(3, chips)

    @pl.when(q >= c)
    def _():
        for s in range(nsub):
            u_side(s).start()

        each(1, early, lambda d: u_out(d, 0).start())

    each(1, n_cols, lambda k: lz_out(k).start())

    for i in range(tiles):
        for p in range(2):
            a, b = split(row_ref[i, p])
            at = pl.ds(p * half + i * ranks, ranks)
            xh[at, :] = a
            xl[at, :] = b

    pos = c * wc + lax.broadcasted_iota(jnp.int32, (wc, ranks), 0)
    parts = []
    for i in range(tiles):
        hit = pos == piv_ref[i:i + 1, :]
        for p in range(2):
            parts.append(jnp.sum(jnp.where(hit, col_ref[i, p], 0.0), axis=0, keepdims=True))
    parts.append(jnp.zeros((eb.shape[1] - 2 * tiles, ranks), jnp.float32))
    eb[c] = jnp.concatenate(parts, axis=0)
    each(1, n_cols, lambda k: e_out(k).start())
    for copy in own:
        copy.wait()

    total = chips * nsub * 2
    per = 2 * (chips - 1)
    own_end = 2 * nsub
    last_phase = own_end + (nsub - 1) * per
    spread_at = jnp.where(c == 0, own_end, 1)
    final_at = last_phase + jnp.where(
        q == c, 0, 2 * jnp.where(c > q, chips - 1 - c, chips - 2 - c) + 1
    )
    final_at = jnp.where(c == 0, total, final_at)

    def finish():
        each(1, n_cols, lambda k: rcopy(
            eb.at[(c + k) % n_cols], eb.at[(c + k) % n_cols], e_send.at[k], e_recv.at[(c + k) % n_cols], sib
        ).wait_recv())
        entries = jnp.sum(eb[...], axis=0)
        lines = []
        levels = lax.broadcasted_iota(jnp.int32, (1, ranks), 1)
        for i in range(tiles):
            er, ei = entries[2 * i:2 * i + 1], entries[2 * i + 1:2 * i + 2]
            keep = (levels < RANK_STEP * rank_ref[i]).astype(jnp.float32)
            mag = jnp.maximum(er * er + ei * ei, 1.0)
            lines.append(keep * er / mag)
            lines.append(-keep * ei / mag)
        lines.append(jnp.zeros((128 - 2 * tiles, ranks), jnp.float32))
        turned = jnp.concatenate(lines, axis=0).T
        for i in range(tiles):
            fr, fi = turned[:, 2 * i:2 * i + 1], turned[:, 2 * i + 1:2 * i + 2]
            lr, li = i * ranks, half + i * ranks
            vr, vi = [], []
            for hh in range(2):
                for s in range(nsub):
                    vr.append(ps[2 * c + hh, s, lr:lr + ranks, :])
                    vi.append(ps[2 * c + hh, s, li:li + ranks, :])
            vr, vi = jnp.concatenate(vr, axis=1), jnp.concatenate(vi, axis=1)
            wr = vr * fr - vi * fi
            wi = vr * fi + vi * fr
            panel_ref[i, 0] = wr
            panel_ref[i, 1] = wi
            a, b = split(wr)
            ch[lr:lr + ranks, :] = a
            cl[lr:lr + ranks, :] = b
            a, b = split(wi)
            ch[li:li + ranks, :] = a
            cl[li:li + ranks, :] = b

        pltpu.make_async_copy(lz, lg.at[h, q], lg_loc.at[0]).wait()
        each(0, chips, lambda o: rcopy(
            lz, lg.at[1 - h, o], lg_sib.at[0], lg_recv.at[1 - h, o], sib
        ).wait_recv())

        def core(k0, carry):
            k = (k0 + 1) % n_cols
            j = (c + k) % n_cols
            lr = lg[0, :, j].reshape(wc, lz.shape[2])
            li = lg[1, :, j].reshape(wc, lz.shape[2])
            rank2 = lz.shape[2]
            uh, ul = split(jnp.concatenate([lr, li], axis=1))
            prod = dot3(ch[...], cl[...], uh, ul)
            real = prod[:half, :rank2] - prod[half:, rank2:]
            imag = prod[:half, rank2:] + prod[half:, :rank2]
            for i in range(tiles):
                ks[k, i, 0] = real[i * ranks:(i + 1) * ranks]
                ks[k, i, 1] = imag[i * ranks:(i + 1) * ranks]

            @pl.when(k > 0)
            def _():
                k_out(k).start()

            return carry

        lax.fori_loop(0, n_cols, core, 0)

    def unit(u, carry):
        later = jnp.maximum(u - own_end, 0)
        index = (later // 2) % (chips - 1)
        down = chips - 1 - index
        down = jnp.where(down > q, down, down - 1)
        t = jnp.where(u < own_end, q, jnp.where(u < last_phase, ahead(index + 1), down))
        s = jnp.where(u < own_end, u // 2, later // per)
        e = u % 2
        b = t * 2 + (h + e) % 2

        @pl.when(u == spread_at)
        def _():
            lz_own.wait()
            each(1, n_cols, lambda k: rcopy(
                lz.at[(c + k) % n_cols], lz.at[(c + k) % n_cols], lz_send.at[k], lz_recv.at[(c + k) % n_cols], sib
            ).wait_recv())
            lg_side().start()
            pltpu.make_async_copy(lz, lg.at[h, q], lg_loc.at[0]).start()
            each(1, chips, lambda d2: lg_out(d2).start())

            @pl.when(q >= c)
            def _():
                each(early, chips, lambda d2: u_out(d2, 0).start())
                for s2 in range(1, nsub):
                    each(1, chips, lambda d2: u_out(d2, s2).start())

        @pl.when(u == last_phase)
        def _():
            def pass_on(d2):
                o = ahead(d2)
                rcopy(lz, lg.at[h, o], lg_send.at[d2], lg_recv.at[h, o], sib).wait_recv()
                lg_forward(d2).start()

            each(1, chips, pass_on)

        @pl.when(jnp.logical_and(t >= c, u < total))
        def _():
            @pl.when(jnp.logical_or(u >= own_end, e > 0))
            def _():
                u_forward(t, s, b).wait_recv()

            @pl.when(jnp.logical_and(u >= own_end, e == 0))
            def _():
                u_forward(t, s, b).start()

            ur, ui = us[b, s, 0], us[b, s, 1]
            uh, ul = split(jnp.concatenate([ur, ui], axis=1))
            prod = dot3(xh[...], xl[...], uh, ul)
            fin[0:half] = prod[:half, :sw] - prod[half:, sw:]
            fin[half:2 * half] = prod[:half, sw:] + prod[half:, :sw]

            @pl.when(c > 0)
            def _():
                rcopy(ps.at[b, s], pr.at[b, s], p_send.at[b, s], p_recv.at[b, s], sib).wait_recv()
                ps[b, s] = fin[...] + pr[b, s]

            @pl.when(c == 0)
            def _():
                ps[b, s] = fin[...]

            @pl.when(t > c)
            def _():
                p_up(b, s).start()

        @pl.when(u == final_at)
        def _():
            finish()

        return carry

    lax.fori_loop(0, total + 1, unit, 0)
    cores_ref[:, 0] = ks[0]

    def gather(k):
        o = (c + k) % n_cols
        rcopy(ks.at[k], kr.at[o], k_send.at[k], k_recv.at[o], sib).wait_recv()
        cores_ref[:, 0] = cores_ref[:, 0] + kr[o]

    each(1, n_cols, gather)

    @pl.when(q >= c)
    def _():
        for s in range(nsub):
            u_side(s).wait_send()

        def left(d):
            for s in range(nsub):
                u_out(d, s).wait_send()

        each(1, chips, left)

    def rest(d):
        t = ahead(d)

        @pl.when(jnp.logical_and(t >= c, d > 0))
        def _():
            for s in range(nsub):
                u_forward(t, s, t * 2 + h).wait_send()

        @pl.when(t > c)
        def _():
            for s in range(nsub):
                for e in range(2):
                    p_up(t * 2 + e, s).wait_send()

        @pl.when(d > 0)
        def _():
            lg_out(d).wait_send()
            lg_forward(d).wait_send()

    each(0, chips, rest)
    lg_side().wait_send()

    def tail(k):
        lz_out(k).wait_send()
        k_out(k).wait_send()
        e_out(k).wait_send()

    each(1, n_cols, tail)


def on_device(n_rows, n_cols, col_samples, row_samples, pivot_rows, rank_blocks, upper_inverse, upanel_left):
    tiles, _, ranks, wc = row_samples.shape
    wr = upper_inverse.shape[2]
    left_ranks = upanel_left.shape[3]
    chips = n_rows // 2
    if chips != n_cols or wc != 2 * wr:
        raise ValueError("unsupported mesh")
    nsub = max(wr // 128, 1)
    sw = wr // nsub
    wq = wc // chips
    m = 2 * tiles * ranks
    f32, bf16 = jnp.float32, jnp.bfloat16
    dma = pltpu.SemaphoreType.DMA
    vmem = pl.BlockSpec(memory_space=pltpu.VMEM)
    hbm = pl.BlockSpec(memory_space=pl.ANY)
    return pl.pallas_call(
        functools.partial(kernel, n_rows, n_cols),
        out_shape=(
            jax.ShapeDtypeStruct((tiles, 2, ranks, wc), f32),
            jax.ShapeDtypeStruct((tiles, 1, 2, ranks, left_ranks), f32),
        ),
        in_specs=[vmem, hbm, hbm, vmem, vmem, pl.BlockSpec(memory_space=pltpu.SMEM)],
        out_specs=(vmem, vmem),
        scratch_shapes=[
            pltpu.VMEM((m, wc), bf16),
            pltpu.VMEM((m, wc), bf16),
            pltpu.VMEM((m, wc), bf16),
            pltpu.VMEM((m, wc), bf16),
            pltpu.VMEM((n_rows, nsub, 2, wc, sw), f32),
            pltpu.VMEM((n_rows, nsub, m, sw), f32),
            pltpu.VMEM((n_rows, nsub, m, sw), f32),
            pltpu.VMEM((m, sw), f32),
            pltpu.VMEM((n_cols, wq, left_ranks), f32),
            pltpu.VMEM((2, chips, n_cols, wq, left_ranks), f32),
            pltpu.VMEM((n_cols, tiles, 2, ranks, left_ranks), f32),
            pltpu.VMEM((n_cols, tiles, 2, ranks, left_ranks), f32),
            pltpu.VMEM((n_cols, -(-2 * tiles // 8) * 8, ranks), f32),
            dma((nsub,)), dma((chips, nsub)), dma((nsub,)), dma((chips, nsub)), dma((n_rows, nsub)),
            dma((n_rows, nsub)), dma((n_rows, nsub)),
            dma((1,)), dma((n_cols,)), dma((n_cols,)), dma((1,)), dma((chips,)), dma((1,)), dma((chips,)),
            dma((2, chips)),
            dma((n_cols,)), dma((n_cols,)), dma((n_cols,)), dma((n_cols,)),
        ],
        compiler_params=pltpu.CompilerParams(
            collective_id=0, has_side_effects=True, vmem_limit_bytes=56 * 1024 * 1024
        ),
    )(row_samples, upper_inverse, upanel_left, col_samples, pivot_rows, rank_blocks)


def solution(mesh):
    in_specs = (
        P("row", None, "col", None),
        P("row", None, None, "col"),
        P("row", None),
        P("row"),
        P(None, "col", "row"),
        P("col", None, None, None),
    )
    out_specs = (P("row", None, None, "col"), P("row", "col", None, None, None))
    body = functools.partial(on_device, mesh.shape["row"], mesh.shape["col"])
    return jax.shard_map(body, mesh=mesh, in_specs=in_specs, out_specs=out_specs, check_vma=False)
```

```python
import functools
import math

import jax
import jax.numpy as jnp
from jax import lax
from jax.experimental import pallas as pl
from jax.experimental.pallas import tpu as pltpu
from jax.sharding import PartitionSpec as P

RANK_STEP = 16
MESH = pl.DeviceIdType.MESH


def split(x):
    high = x.astype(jnp.bfloat16)
    low = (x - high.astype(jnp.float32)).astype(jnp.bfloat16)
    return high, low


def dot3(xh, xl, uh, ul):
    def single(a, b):
        return jnp.dot(a, b, preferred_element_type=jnp.float32)

    return single(xh, uh) + (single(xh, ul) + single(xl, uh))


def kernel(
    n_rows, n_cols,
    row_ref, u_ref, up_ref, col_ref, piv_ref, rank_ref,
    panel_ref, cores_ref,
    xh, xl, ch, cl, us, ps, pr, fin, lz, lg, ks, kr, eb,
    u_loc, u_send, u_sib, u_fwd, u_recv,
    p_send, p_recv,
    lz_loc, lz_send, lz_recv, lg_loc, lg_send, lg_sib, lg_fwd, lg_recv,
    k_send, k_recv, e_send, e_recv,
):
    r, c = lax.axis_index("row"), lax.axis_index("col")
    chips = n_rows // 2
    nx = math.isqrt(chips)
    ny = chips // nx
    q, h = r // 2, r % 2
    qy, qx = q // nx, q % nx
    tiles, _, ranks, wc = row_ref.shape
    nsub, sw = us.shape[1], us.shape[4]
    wq = lz.shape[1]
    half = tiles * ranks
    sib = (q * 2 + 1 - h, c)

    def ahead(d):
        return ((qy + d // nx) % ny) * nx + (qx + d % nx) % nx

    def behind(d):
        return ((qy + ny - d // nx) % ny) * nx + (qx + nx - d % nx) % nx

    def rcopy(src, dst, ssem, rsem, dev):
        return pltpu.make_async_remote_copy(
            src_ref=src, dst_ref=dst, send_sem=ssem, recv_sem=rsem, device_id=dev, device_id_type=MESH
        )

    def u_out(d, s):
        return rcopy(
            u_ref.at[:, :, s * sw:(s + 1) * sw], us.at[r, s], u_send.at[d, s], u_recv.at[r, s],
            (behind(d) * 2 + h, c),
        )

    def u_side(s):
        return rcopy(u_ref.at[:, :, s * sw:(s + 1) * sw], us.at[r, s], u_sib.at[s], u_recv.at[r, s], sib)

    def u_forward(t, s, b):
        return rcopy(us.at[b, s], us.at[b, s], u_fwd.at[t, s], u_recv.at[b, s], sib)

    def u_relay(s, b):
        to = behind(1) if s % 2 == 0 else behind(2)
        return rcopy(us.at[b, s], us.at[b, s], u_send.at[chips - 1, s], u_recv.at[b, s], (to * 2 + h, c))

    def p_up(b, s):
        return rcopy(ps.at[b, s], pr.at[b, s], p_send.at[b, s], p_recv.at[b, s], (r, c + 1))

    def lz_out(k):
        to = (c + k) % n_cols
        start = pl.multiple_of(to * wc + q * wq, wq)
        return rcopy(up_ref.at[0, h, pl.ds(start, wq), :], lz.at[c], lz_send.at[k], lz_recv.at[c], (r, to))

    def lg_out(d):
        return rcopy(lz, lg.at[h, q], lg_send.at[d], lg_recv.at[h, q], (behind(d) * 2 + h, c))

    def lg_side():
        return rcopy(lz, lg.at[h, q], lg_sib.at[0], lg_recv.at[h, q], sib)

    def lg_forward(d):
        b = ahead(d)
        return rcopy(lg.at[h, b], lg.at[h, b], lg_fwd.at[d], lg_recv.at[h, b], sib)

    def k_out(k):
        to = (c + k) % n_cols
        return rcopy(ks.at[k], kr.at[c], k_send.at[k], k_recv.at[c], (r, to))

    def e_out(k):
        return rcopy(eb.at[c], eb.at[c], e_send.at[k], e_recv.at[c], (r, (c + k) % n_cols))

    def each(first, last, body):
        lax.fori_loop(first, last, lambda i, z: (body(i), z)[1], 0)

    own = [
        pltpu.make_async_copy(u_ref.at[:, :, s * sw:(s + 1) * sw], us.at[r, s], u_loc.at[s]) for s in range(nsub)
    ]
    for copy in own:
        copy.start()
    mine = pl.multiple_of(c * wc + q * wq, wq)
    lz_own = pltpu.make_async_copy(up_ref.at[0, h, pl.ds(mine, wq), :], lz.at[c], lz_loc.at[0])
    lz_own.start()
    barrier = pltpu.get_barrier_semaphore()

    def signal(dev):
        pl.semaphore_signal(barrier, inc=1, device_id=dev, device_id_type=MESH)

    signal(sib)
    each(1, chips, lambda d: signal((behind(d) * 2 + h, c)))
    each(1, n_cols, lambda k: signal((r, (c + k) % n_cols)))
    pl.semaphore_wait(barrier, 1 + (chips - 1) + (n_cols - 1))

    square = nx == 2 and ny == 2
    direct = chips - 1 if square else chips

    @pl.when(q >= c)
    def _():
        for s in range(nsub):
            u_side(s).start()

        for s in range(nsub):
            each(1, direct, lambda d: u_out(d, s).start())

    each(1, n_cols, lambda k: lz_out(k).start())

    for i in range(tiles):
        for p in range(2):
            a, b = split(row_ref[i, p])
            at = pl.ds(p * half + i * ranks, ranks)
            xh[at, :] = a
            xl[at, :] = b

    pos = c * wc + lax.broadcasted_iota(jnp.int32, (wc, ranks), 0)
    parts = []
    for i in range(tiles):
        hit = pos == piv_ref[i:i + 1, :]
        for p in range(2):
            parts.append(jnp.sum(jnp.where(hit, col_ref[i, p], 0.0), axis=0, keepdims=True))
    parts.append(jnp.zeros((eb.shape[1] - 2 * tiles, ranks), jnp.float32))
    eb[c] = jnp.concatenate(parts, axis=0)
    each(1, n_cols, lambda k: e_out(k).start())
    for copy in own:
        copy.wait()

    total = chips * nsub * 2
    per = 2 * (chips - 1)
    own_end = 2 * nsub
    last_phase = own_end + (nsub - 1) * per
    spread_at = jnp.where(c == 0, own_end, 0)
    final_at = last_phase + jnp.where(
        q == c, 0, 2 * jnp.where(c > q, chips - 1 - c, chips - 2 - c) + 1
    )
    final_at = jnp.where(c == 0, total, final_at)

    def finish():
        each(1, n_cols, lambda k: rcopy(
            eb.at[(c + k) % n_cols], eb.at[(c + k) % n_cols], e_send.at[k], e_recv.at[(c + k) % n_cols], sib
        ).wait_recv())
        entries = jnp.sum(eb[...], axis=0)
        lines = []
        levels = lax.broadcasted_iota(jnp.int32, (1, ranks), 1)
        for i in range(tiles):
            er, ei = entries[2 * i:2 * i + 1], entries[2 * i + 1:2 * i + 2]
            keep = (levels < RANK_STEP * rank_ref[i]).astype(jnp.float32)
            mag = jnp.maximum(er * er + ei * ei, 1.0)
            lines.append(keep * er / mag)
            lines.append(-keep * ei / mag)
        lines.append(jnp.zeros((128 - 2 * tiles, ranks), jnp.float32))
        turned = jnp.concatenate(lines, axis=0).T
        for i in range(tiles):
            fr, fi = turned[:, 2 * i:2 * i + 1], turned[:, 2 * i + 1:2 * i + 2]
            lr, li = i * ranks, half + i * ranks
            vr, vi = [], []
            for hh in range(2):
                for s in range(nsub):
                    vr.append(ps[2 * c + hh, s, lr:lr + ranks, :])
                    vi.append(ps[2 * c + hh, s, li:li + ranks, :])
            vr, vi = jnp.concatenate(vr, axis=1), jnp.concatenate(vi, axis=1)
            wr = vr * fr - vi * fi
            wi = vr * fi + vi * fr
            panel_ref[i, 0] = wr
            panel_ref[i, 1] = wi
            a, b = split(wr)
            ch[lr:lr + ranks, :] = a
            cl[lr:lr + ranks, :] = b
            a, b = split(wi)
            ch[li:li + ranks, :] = a
            cl[li:li + ranks, :] = b

        pltpu.make_async_copy(lz, lg.at[h, q], lg_loc.at[0]).wait()
        each(0, chips, lambda o: rcopy(
            lz, lg.at[1 - h, o], lg_sib.at[0], lg_recv.at[1 - h, o], sib
        ).wait_recv())

        def core(k0, carry):
            k = (k0 + 1) % n_cols
            j = (c + k) % n_cols
            lr = lg[0, :, j].reshape(wc, lz.shape[2])
            li = lg[1, :, j].reshape(wc, lz.shape[2])
            rank2 = lz.shape[2]
            uh, ul = split(jnp.concatenate([lr, li], axis=1))
            prod = dot3(ch[...], cl[...], uh, ul)
            real = prod[:half, :rank2] - prod[half:, rank2:]
            imag = prod[:half, rank2:] + prod[half:, :rank2]
            for i in range(tiles):
                ks[k, i, 0] = real[i * ranks:(i + 1) * ranks]
                ks[k, i, 1] = imag[i * ranks:(i + 1) * ranks]

            @pl.when(k > 0)
            def _():
                k_out(k).start()

            return carry

        lax.fori_loop(0, n_cols, core, 0)

    def unit(u, carry):
        later = jnp.maximum(u - own_end, 0)
        index = (later // 2) % (chips - 1)
        down = chips - 1 - index
        down = jnp.where(down > q, down, down - 1)
        t = jnp.where(u < own_end, q, jnp.where(u < last_phase, ahead(index + 1), down))
        s = jnp.where(u < own_end, u // 2, later // per)
        e = u % 2
        b = t * 2 + (h + e) % 2

        @pl.when(u == spread_at)
        def _():
            lz_own.wait()
            each(1, n_cols, lambda k: rcopy(
                lz.at[(c + k) % n_cols], lz.at[(c + k) % n_cols], lz_send.at[k], lz_recv.at[(c + k) % n_cols], sib
            ).wait_recv())
            lg_side().start()
            pltpu.make_async_copy(lz, lg.at[h, q], lg_loc.at[0]).start()
            each(1, chips, lambda d2: lg_out(d2).start())

        @pl.when(u == last_phase)
        def _():
            def pass_on(d2):
                o = ahead(d2)
                rcopy(lz, lg.at[h, o], lg_send.at[d2], lg_recv.at[h, o], sib).wait_recv()
                lg_forward(d2).start()

            each(1, chips, pass_on)

        @pl.when(jnp.logical_and(t >= c, u < total))
        def _():
            @pl.when(jnp.logical_or(u >= own_end, e > 0))
            def _():
                u_forward(t, s, b).wait_recv()

            @pl.when(jnp.logical_and(u >= own_end, e == 0))
            def _():
                u_forward(t, s, b).start()

            if square:
                for s2 in range(nsub):
                    source = ahead(2 - s2 % 2)

                    @pl.when(jnp.logical_and(jnp.logical_and(u >= own_end, e == 0), jnp.logical_and(s == s2, t == source)))
                    def _():
                        u_relay(s2, source * 2 + h).start()

            ur, ui = us[b, s, 0], us[b, s, 1]
            uh, ul = split(jnp.concatenate([ur, ui], axis=1))
            prod = dot3(xh[...], xl[...], uh, ul)
            fin[0:half] = prod[:half, :sw] - prod[half:, sw:]
            fin[half:2 * half] = prod[:half, sw:] + prod[half:, :sw]

            @pl.when(c > 0)
            def _():
                rcopy(ps.at[b, s], pr.at[b, s], p_send.at[b, s], p_recv.at[b, s], sib).wait_recv()
                ps[b, s] = fin[...] + pr[b, s]

            @pl.when(c == 0)
            def _():
                ps[b, s] = fin[...]

            @pl.when(t > c)
            def _():
                p_up(b, s).start()

        @pl.when(u == final_at)
        def _():
            finish()

        return carry

    lax.fori_loop(0, total + 1, unit, 0)
    cores_ref[:, 0] = ks[0]

    def gather(k):
        o = (c + k) % n_cols
        rcopy(ks.at[k], kr.at[o], k_send.at[k], k_recv.at[o], sib).wait_recv()
        cores_ref[:, 0] = cores_ref[:, 0] + kr[o]

    each(1, n_cols, gather)

    @pl.when(q >= c)
    def _():
        for s in range(nsub):
            u_side(s).wait_send()

        def left(d):
            for s in range(nsub):
                u_out(d, s).wait_send()

        each(1, direct, left)

    if square:
        for s in range(nsub):
            source = ahead(2 - s % 2)

            @pl.when(source >= c)
            def _():
                u_relay(s, source * 2 + h).wait_send()

    def rest(d):
        t = ahead(d)

        @pl.when(jnp.logical_and(t >= c, d > 0))
        def _():
            for s in range(nsub):
                u_forward(t, s, t * 2 + h).wait_send()

        @pl.when(t > c)
        def _():
            for s in range(nsub):
                for e in range(2):
                    p_up(t * 2 + e, s).wait_send()

        @pl.when(d > 0)
        def _():
            lg_out(d).wait_send()
            lg_forward(d).wait_send()

    each(0, chips, rest)
    lg_side().wait_send()

    def tail(k):
        lz_out(k).wait_send()
        k_out(k).wait_send()
        e_out(k).wait_send()

    each(1, n_cols, tail)


def on_device(n_rows, n_cols, col_samples, row_samples, pivot_rows, rank_blocks, upper_inverse, upanel_left):
    tiles, _, ranks, wc = row_samples.shape
    wr = upper_inverse.shape[2]
    left_ranks = upanel_left.shape[3]
    chips = n_rows // 2
    if chips != n_cols or wc != 2 * wr:
        raise ValueError("unsupported mesh")
    nsub = max(wr // 128, 1)
    sw = wr // nsub
    wq = wc // chips
    m = 2 * tiles * ranks
    f32, bf16 = jnp.float32, jnp.bfloat16
    dma = pltpu.SemaphoreType.DMA
    vmem = pl.BlockSpec(memory_space=pltpu.VMEM)
    hbm = pl.BlockSpec(memory_space=pl.ANY)
    return pl.pallas_call(
        functools.partial(kernel, n_rows, n_cols),
        out_shape=(
            jax.ShapeDtypeStruct((tiles, 2, ranks, wc), f32),
            jax.ShapeDtypeStruct((tiles, 1, 2, ranks, left_ranks), f32),
        ),
        in_specs=[vmem, hbm, hbm, vmem, vmem, pl.BlockSpec(memory_space=pltpu.SMEM)],
        out_specs=(vmem, vmem),
        scratch_shapes=[
            pltpu.VMEM((m, wc), bf16),
            pltpu.VMEM((m, wc), bf16),
            pltpu.VMEM((m, wc), bf16),
            pltpu.VMEM((m, wc), bf16),
            pltpu.VMEM((n_rows, nsub, 2, wc, sw), f32),
            pltpu.VMEM((n_rows, nsub, m, sw), f32),
            pltpu.VMEM((n_rows, nsub, m, sw), f32),
            pltpu.VMEM((m, sw), f32),
            pltpu.VMEM((n_cols, wq, left_ranks), f32),
            pltpu.VMEM((2, chips, n_cols, wq, left_ranks), f32),
            pltpu.VMEM((n_cols, tiles, 2, ranks, left_ranks), f32),
            pltpu.VMEM((n_cols, tiles, 2, ranks, left_ranks), f32),
            pltpu.VMEM((n_cols, -(-2 * tiles // 8) * 8, ranks), f32),
            dma((nsub,)), dma((chips, nsub)), dma((nsub,)), dma((chips, nsub)), dma((n_rows, nsub)),
            dma((n_rows, nsub)), dma((n_rows, nsub)),
            dma((1,)), dma((n_cols,)), dma((n_cols,)), dma((1,)), dma((chips,)), dma((1,)), dma((chips,)),
            dma((2, chips)),
            dma((n_cols,)), dma((n_cols,)), dma((n_cols,)), dma((n_cols,)),
        ],
        compiler_params=pltpu.CompilerParams(
            collective_id=0, has_side_effects=True, vmem_limit_bytes=56 * 1024 * 1024
        ),
    )(row_samples, upper_inverse, upanel_left, col_samples, pivot_rows, rank_blocks)


def solution(mesh):
    in_specs = (
        P("row", None, "col", None),
        P("row", None, None, "col"),
        P("row", None),
        P("row"),
        P(None, "col", "row"),
        P("col", None, None, None),
    )
    out_specs = (P("row", None, None, "col"), P("row", "col", None, None, None))
    body = functools.partial(on_device, mesh.shape["row"], mesh.shape["col"])
    return jax.shard_map(body, mesh=mesh, in_specs=in_specs, out_specs=out_specs, check_vma=False)
```

```python
import functools
import math

import jax
import jax.numpy as jnp
from jax import lax
from jax.experimental import pallas as pl
from jax.experimental.pallas import tpu as pltpu
from jax.sharding import PartitionSpec as P

RANK_STEP = 16
MESH = pl.DeviceIdType.MESH


def split(x):
    high = x.astype(jnp.bfloat16)
    low = (x - high.astype(jnp.float32)).astype(jnp.bfloat16)
    return high, low


def dot3(xh, xl, uh, ul):
    def single(a, b):
        return jnp.dot(a, b, preferred_element_type=jnp.float32)

    return single(xh, uh) + (single(xh, ul) + single(xl, uh))


def kernel(
    n_rows, n_cols,
    row_ref, u_ref, up_ref, col_ref, piv_ref, rank_ref,
    panel_ref, cores_ref,
    xh, xl, ch, cl, us, ps, pr, fin, lz, lg, ks, kr, eb,
    u_loc, u_send, u_sib, u_fwd, u_recv,
    p_send, p_recv,
    lz_loc, lz_send, lz_recv, lg_loc, lg_send, lg_sib, lg_fwd, lg_recv,
    k_send, k_recv, e_send, e_recv,
):
    r, c = lax.axis_index("row"), lax.axis_index("col")
    chips = n_rows // 2
    nx = math.isqrt(chips)
    ny = chips // nx
    q, h = r // 2, r % 2
    qy, qx = q // nx, q % nx
    tiles, _, ranks, wc = row_ref.shape
    nsub, sw = us.shape[1], us.shape[4]
    wq = lz.shape[1]
    half = tiles * ranks
    sib = (q * 2 + 1 - h, c)

    def ahead(d):
        return ((qy + d // nx) % ny) * nx + (qx + d % nx) % nx

    def behind(d):
        return ((qy + ny - d // nx) % ny) * nx + (qx + nx - d % nx) % nx

    def rcopy(src, dst, ssem, rsem, dev):
        return pltpu.make_async_remote_copy(
            src_ref=src, dst_ref=dst, send_sem=ssem, recv_sem=rsem, device_id=dev, device_id_type=MESH
        )

    def u_out(d, s):
        return rcopy(
            u_ref.at[:, :, s * sw:(s + 1) * sw], us.at[r, s], u_send.at[d, s], u_recv.at[r, s],
            (behind(d) * 2 + h, c),
        )

    def u_side(s):
        return rcopy(u_ref.at[:, :, s * sw:(s + 1) * sw], us.at[r, s], u_sib.at[s], u_recv.at[r, s], sib)

    def u_forward(t, s, b):
        return rcopy(us.at[b, s], us.at[b, s], u_fwd.at[t, s], u_recv.at[b, s], sib)

    def p_up(b, s):
        return rcopy(ps.at[b, s], pr.at[b, s], p_send.at[b, s], p_recv.at[b, s], (r, c + 1))

    def lz_out(k):
        to = (c + k) % n_cols
        start = pl.multiple_of(to * wc + q * wq, wq)
        return rcopy(up_ref.at[0, h, pl.ds(start, wq), :], lz.at[c], lz_send.at[k], lz_recv.at[c], (r, to))

    def lg_out(d):
        return rcopy(lz, lg.at[h, q], lg_send.at[d], lg_recv.at[h, q], (behind(d) * 2 + h, c))

    def lg_side():
        return rcopy(lz, lg.at[h, q], lg_sib.at[0], lg_recv.at[h, q], sib)

    def lg_forward(d):
        b = ahead(d)
        return rcopy(lg.at[h, b], lg.at[h, b], lg_fwd.at[d], lg_recv.at[h, b], sib)

    def k_out(k):
        to = (c + k) % n_cols
        return rcopy(ks.at[k], kr.at[c], k_send.at[k], k_recv.at[c], (r, to))

    def e_out(k):
        return rcopy(eb.at[c], eb.at[c], e_send.at[k], e_recv.at[c], (r, (c + k) % n_cols))

    def each(first, last, body):
        lax.fori_loop(first, last, lambda i, z: (body(i), z)[1], 0)

    own = [
        pltpu.make_async_copy(u_ref.at[:, :, s * sw:(s + 1) * sw], us.at[r, s], u_loc.at[s]) for s in range(nsub)
    ]
    for copy in own:
        copy.start()
    mine = pl.multiple_of(c * wc + q * wq, wq)
    lz_own = pltpu.make_async_copy(up_ref.at[0, h, pl.ds(mine, wq), :], lz.at[c], lz_loc.at[0])
    lz_own.start()
    barrier = pltpu.get_barrier_semaphore()

    def signal(dev):
        pl.semaphore_signal(barrier, inc=1, device_id=dev, device_id_type=MESH)

    signal(sib)
    each(1, chips, lambda d: signal((behind(d) * 2 + h, c)))
    each(1, n_cols, lambda k: signal((r, (c + k) % n_cols)))
    pl.semaphore_wait(barrier, 1 + (chips - 1) + (n_cols - 1))

    @pl.when(q >= c)
    def _():
        for s in range(nsub):
            u_side(s).start()

        for s in range(nsub):
            each(1, chips, lambda d: u_out(d, s).start())

    each(1, n_cols, lambda k: lz_out(k).start())

    for i in range(tiles):
        for p in range(2):
            a, b = split(row_ref[i, p])
            at = pl.ds(p * half + i * ranks, ranks)
            xh[at, :] = a
            xl[at, :] = b

    pos = c * wc + lax.broadcasted_iota(jnp.int32, (wc, ranks), 0)
    parts = []
    for i in range(tiles):
        hit = pos == piv_ref[i:i + 1, :]
        for p in range(2):
            parts.append(jnp.sum(jnp.where(hit, col_ref[i, p], 0.0), axis=0, keepdims=True))
    parts.append(jnp.zeros((eb.shape[1] - 2 * tiles, ranks), jnp.float32))
    eb[c] = jnp.concatenate(parts, axis=0)
    each(1, n_cols, lambda k: e_out(k).start())
    for copy in own:
        copy.wait()

    near = chips * (nsub - 1)
    total = 2 * (near + chips + nsub - 1)
    spread_at = jnp.where(c == 0, 2, 0)
    final_at = jnp.where(c == 0, total - 1, 2 * (near + chips - 1 - c) + 1)

    def finish():
        def pass_on(d2):
            o = ahead(d2)
            rcopy(lz, lg.at[h, o], lg_send.at[d2], lg_recv.at[h, o], sib).wait_recv()
            lg_forward(d2).start()

        each(1, chips, pass_on)

        each(1, n_cols, lambda k: rcopy(
            eb.at[(c + k) % n_cols], eb.at[(c + k) % n_cols], e_send.at[k], e_recv.at[(c + k) % n_cols], sib
        ).wait_recv())
        entries = jnp.sum(eb[...], axis=0)
        lines = []
        levels = lax.broadcasted_iota(jnp.int32, (1, ranks), 1)
        for i in range(tiles):
            er, ei = entries[2 * i:2 * i + 1], entries[2 * i + 1:2 * i + 2]
            keep = (levels < RANK_STEP * rank_ref[i]).astype(jnp.float32)
            mag = jnp.maximum(er * er + ei * ei, 1.0)
            lines.append(keep * er / mag)
            lines.append(-keep * ei / mag)
        lines.append(jnp.zeros((128 - 2 * tiles, ranks), jnp.float32))
        turned = jnp.concatenate(lines, axis=0).T
        for i in range(tiles):
            fr, fi = turned[:, 2 * i:2 * i + 1], turned[:, 2 * i + 1:2 * i + 2]
            lr, li = i * ranks, half + i * ranks
            vr, vi = [], []
            for hh in range(2):
                for s in range(nsub):
                    vr.append(ps[2 * c + hh, s, lr:lr + ranks, :])
                    vi.append(ps[2 * c + hh, s, li:li + ranks, :])
            vr, vi = jnp.concatenate(vr, axis=1), jnp.concatenate(vi, axis=1)
            wr = vr * fr - vi * fi
            wi = vr * fi + vi * fr
            panel_ref[i, 0] = wr
            panel_ref[i, 1] = wi
            a, b = split(wr)
            ch[lr:lr + ranks, :] = a
            cl[lr:lr + ranks, :] = b
            a, b = split(wi)
            ch[li:li + ranks, :] = a
            cl[li:li + ranks, :] = b

        pltpu.make_async_copy(lz, lg.at[h, q], lg_loc.at[0]).wait()
        each(0, chips, lambda o: rcopy(
            lz, lg.at[1 - h, o], lg_sib.at[0], lg_recv.at[1 - h, o], sib
        ).wait_recv())

        def core(k0, carry):
            k = (k0 + 1) % n_cols
            j = (c + k) % n_cols
            lr = lg[0, :, j].reshape(wc, lz.shape[2])
            li = lg[1, :, j].reshape(wc, lz.shape[2])
            rank2 = lz.shape[2]
            uh, ul = split(jnp.concatenate([lr, li], axis=1))
            prod = dot3(ch[...], cl[...], uh, ul)
            real = prod[:half, :rank2] - prod[half:, rank2:]
            imag = prod[:half, rank2:] + prod[half:, :rank2]
            for i in range(tiles):
                ks[k, i, 0] = real[i * ranks:(i + 1) * ranks]
                ks[k, i, 1] = imag[i * ranks:(i + 1) * ranks]

            @pl.when(k > 0)
            def _():
                k_out(k).start()

            return carry

        lax.fori_loop(0, n_cols, core, 0)

    def unit(u, carry):
        slot = u // 2
        t = jnp.where(slot < near, ahead(slot % chips), jnp.maximum(near + chips - 1 - slot, 0))
        s = jnp.where(slot < near, slot // chips, jnp.where(slot < near + chips, nsub - 1, slot - near - chips))
        live = jnp.logical_and(t >= c, jnp.logical_or(slot >= near, t > 0))
        e = u % 2
        b = t * 2 + (h + e) % 2

        @pl.when(u == spread_at)
        def _():
            lz_own.wait()
            each(1, n_cols, lambda k: rcopy(
                lz.at[(c + k) % n_cols], lz.at[(c + k) % n_cols], lz_send.at[k], lz_recv.at[(c + k) % n_cols], sib
            ).wait_recv())
            lg_side().start()
            pltpu.make_async_copy(lz, lg.at[h, q], lg_loc.at[0]).start()
            each(1, chips, lambda d2: lg_out(d2).start())

        @pl.when(live)
        def _():
            @pl.when(jnp.logical_or(t != q, e > 0))
            def _():
                u_forward(t, s, b).wait_recv()

            @pl.when(jnp.logical_and(t != q, e == 0))
            def _():
                u_forward(t, s, b).start()

            ur, ui = us[b, s, 0], us[b, s, 1]
            uh, ul = split(jnp.concatenate([ur, ui], axis=1))
            prod = dot3(xh[...], xl[...], uh, ul)
            fin[0:half] = prod[:half, :sw] - prod[half:, sw:]
            fin[half:2 * half] = prod[:half, sw:] + prod[half:, :sw]

            @pl.when(c > 0)
            def _():
                rcopy(ps.at[b, s], pr.at[b, s], p_send.at[b, s], p_recv.at[b, s], sib).wait_recv()
                ps[b, s] = fin[...] + pr[b, s]

            @pl.when(c == 0)
            def _():
                ps[b, s] = fin[...]

            @pl.when(t > c)
            def _():
                p_up(b, s).start()

        @pl.when(u == final_at)
        def _():
            finish()

        return carry

    lax.fori_loop(0, total, unit, 0)
    cores_ref[:, 0] = ks[0]

    def gather(k):
        o = (c + k) % n_cols
        rcopy(ks.at[k], kr.at[o], k_send.at[k], k_recv.at[o], sib).wait_recv()
        cores_ref[:, 0] = cores_ref[:, 0] + kr[o]

    each(1, n_cols, gather)

    @pl.when(q >= c)
    def _():
        for s in range(nsub):
            u_side(s).wait_send()

        def left(d):
            for s in range(nsub):
                u_out(d, s).wait_send()

        each(1, chips, left)

    def rest(d):
        t = ahead(d)

        @pl.when(jnp.logical_and(t >= c, d > 0))
        def _():
            for s in range(nsub):
                u_forward(t, s, t * 2 + h).wait_send()

        @pl.when(t > c)
        def _():
            for s in range(nsub):
                for e in range(2):
                    p_up(t * 2 + e, s).wait_send()

        @pl.when(d > 0)
        def _():
            lg_out(d).wait_send()
            lg_forward(d).wait_send()

    each(0, chips, rest)
    lg_side().wait_send()

    def tail(k):
        lz_out(k).wait_send()
        k_out(k).wait_send()
        e_out(k).wait_send()

    each(1, n_cols, tail)


def on_device(n_rows, n_cols, col_samples, row_samples, pivot_rows, rank_blocks, upper_inverse, upanel_left):
    tiles, _, ranks, wc = row_samples.shape
    wr = upper_inverse.shape[2]
    left_ranks = upanel_left.shape[3]
    chips = n_rows // 2
    if chips != n_cols or wc != 2 * wr:
        raise ValueError("unsupported mesh")
    nsub = max(wr // 128, 1)
    sw = wr // nsub
    wq = wc // chips
    m = 2 * tiles * ranks
    f32, bf16 = jnp.float32, jnp.bfloat16
    dma = pltpu.SemaphoreType.DMA
    vmem = pl.BlockSpec(memory_space=pltpu.VMEM)
    hbm = pl.BlockSpec(memory_space=pl.ANY)
    return pl.pallas_call(
        functools.partial(kernel, n_rows, n_cols),
        out_shape=(
            jax.ShapeDtypeStruct((tiles, 2, ranks, wc), f32),
            jax.ShapeDtypeStruct((tiles, 1, 2, ranks, left_ranks), f32),
        ),
        in_specs=[vmem, hbm, hbm, vmem, vmem, pl.BlockSpec(memory_space=pltpu.SMEM)],
        out_specs=(vmem, vmem),
        scratch_shapes=[
            pltpu.VMEM((m, wc), bf16),
            pltpu.VMEM((m, wc), bf16),
            pltpu.VMEM((m, wc), bf16),
            pltpu.VMEM((m, wc), bf16),
            pltpu.VMEM((n_rows, nsub, 2, wc, sw), f32),
            pltpu.VMEM((n_rows, nsub, m, sw), f32),
            pltpu.VMEM((n_rows, nsub, m, sw), f32),
            pltpu.VMEM((m, sw), f32),
            pltpu.VMEM((n_cols, wq, left_ranks), f32),
            pltpu.VMEM((2, chips, n_cols, wq, left_ranks), f32),
            pltpu.VMEM((n_cols, tiles, 2, ranks, left_ranks), f32),
            pltpu.VMEM((n_cols, tiles, 2, ranks, left_ranks), f32),
            pltpu.VMEM((n_cols, -(-2 * tiles // 8) * 8, ranks), f32),
            dma((nsub,)), dma((chips, nsub)), dma((nsub,)), dma((chips, nsub)), dma((n_rows, nsub)),
            dma((n_rows, nsub)), dma((n_rows, nsub)),
            dma((1,)), dma((n_cols,)), dma((n_cols,)), dma((1,)), dma((chips,)), dma((1,)), dma((chips,)),
            dma((2, chips)),
            dma((n_cols,)), dma((n_cols,)), dma((n_cols,)), dma((n_cols,)),
        ],
        compiler_params=pltpu.CompilerParams(
            collective_id=0, has_side_effects=True, vmem_limit_bytes=56 * 1024 * 1024
        ),
    )(row_samples, upper_inverse, upanel_left, col_samples, pivot_rows, rank_blocks)


def solution(mesh):
    in_specs = (
        P("row", None, "col", None),
        P("row", None, None, "col"),
        P("row", None),
        P("row"),
        P(None, "col", "row"),
        P("col", None, None, None),
    )
    out_specs = (P("row", None, None, "col"), P("row", "col", None, None, None))
    body = functools.partial(on_device, mesh.shape["row"], mesh.shape["col"])
    return jax.shard_map(body, mesh=mesh, in_specs=in_specs, out_specs=out_specs, check_vma=False)
```

```python
import functools
import math

import jax
import jax.numpy as jnp
from jax import lax
from jax.experimental import pallas as pl
from jax.experimental.pallas import tpu as pltpu
from jax.sharding import PartitionSpec as P

RANK_STEP = 16
MESH = pl.DeviceIdType.MESH


def split(x):
    high = x.astype(jnp.bfloat16)
    low = (x - high.astype(jnp.float32)).astype(jnp.bfloat16)
    return high, low


def dot3(xh, xl, uh, ul):
    def single(a, b):
        return jnp.dot(a, b, preferred_element_type=jnp.float32)

    return single(xh, uh) + (single(xh, ul) + single(xl, uh))


def kernel(
    n_rows, n_cols,
    row_ref, u_ref, up_ref, col_ref, piv_ref, rank_ref,
    panel_ref, cores_ref,
    xh, xl, ch, cl, us, ps, pr, fin, lz, lg, ks, kr, eb,
    u_loc, u_send, u_sib, u_fwd, u_recv,
    p_send, p_recv,
    lz_loc, lz_send, lz_recv, lg_loc, lg_send, lg_sib, lg_fwd, lg_recv,
    k_send, k_recv, e_send, e_recv,
):
    r, c = lax.axis_index("row"), lax.axis_index("col")
    chips = n_rows // 2
    nx = math.isqrt(chips)
    ny = chips // nx
    q, h = r // 2, r % 2
    qy, qx = q // nx, q % nx
    tiles, _, ranks, wc = row_ref.shape
    nsub, sw = us.shape[1], us.shape[4]
    wq = lz.shape[1]
    half = tiles * ranks
    sib = (q * 2 + 1 - h, c)

    def ahead(d):
        return ((qy + d // nx) % ny) * nx + (qx + d % nx) % nx

    def behind(d):
        return ((qy + ny - d // nx) % ny) * nx + (qx + nx - d % nx) % nx

    def rcopy(src, dst, ssem, rsem, dev):
        return pltpu.make_async_remote_copy(
            src_ref=src, dst_ref=dst, send_sem=ssem, recv_sem=rsem, device_id=dev, device_id_type=MESH
        )

    def u_out(d, s):
        return rcopy(
            u_ref.at[:, :, s * sw:(s + 1) * sw], us.at[r, s], u_send.at[d, s], u_recv.at[r, s],
            (behind(d) * 2 + h, c),
        )

    def u_side(s):
        return rcopy(u_ref.at[:, :, s * sw:(s + 1) * sw], us.at[r, s], u_sib.at[s], u_recv.at[r, s], sib)

    def u_forward(t, s, b):
        return rcopy(us.at[b, s], us.at[b, s], u_fwd.at[t, s], u_recv.at[b, s], sib)

    def p_up(b, s):
        return rcopy(ps.at[b, s], pr.at[b, s], p_send.at[b, s], p_recv.at[b, s], (r, c + 1))

    def lz_out(k):
        to = (c + k) % n_cols
        start = pl.multiple_of(to * wc + q * wq, wq)
        return rcopy(up_ref.at[0, h, pl.ds(start, wq), :], lz.at[c], lz_send.at[k], lz_recv.at[c], (r, to))

    def lg_out(d):
        return rcopy(lz, lg.at[h, q], lg_send.at[d], lg_recv.at[h, q], (behind(d) * 2 + h, c))

    def lg_side():
        return rcopy(lz, lg.at[h, q], lg_sib.at[0], lg_recv.at[h, q], sib)

    def lg_forward(d):
        b = ahead(d)
        return rcopy(lg.at[h, b], lg.at[h, b], lg_fwd.at[d], lg_recv.at[h, b], sib)

    def k_out(k):
        to = (c + k) % n_cols
        return rcopy(ks.at[k], kr.at[c], k_send.at[k], k_recv.at[c], (r, to))

    def e_out(k):
        return rcopy(eb.at[c], eb.at[c], e_send.at[k], e_recv.at[c], (r, (c + k) % n_cols))

    def each(first, last, body):
        lax.fori_loop(first, last, lambda i, z: (body(i), z)[1], 0)

    own = [
        pltpu.make_async_copy(u_ref.at[:, :, s * sw:(s + 1) * sw], us.at[r, s], u_loc.at[s]) for s in range(nsub)
    ]
    for copy in own:
        copy.start()
    mine = pl.multiple_of(c * wc + q * wq, wq)
    lz_own = pltpu.make_async_copy(up_ref.at[0, h, pl.ds(mine, wq), :], lz.at[c], lz_loc.at[0])
    lz_own.start()
    barrier = pltpu.get_barrier_semaphore()

    def signal(dev):
        pl.semaphore_signal(barrier, inc=1, device_id=dev, device_id_type=MESH)

    signal(sib)
    each(1, chips, lambda d: signal((behind(d) * 2 + h, c)))
    each(1, n_cols, lambda k: signal((r, (c + k) % n_cols)))
    pl.semaphore_wait(barrier, 1 + (chips - 1) + (n_cols - 1))

    @pl.when(q >= c)
    def _():
        for s in range(nsub):
            u_side(s).start()

        for s in range(nsub):
            each(1, chips, lambda d: u_out(d if s == 0 else chips - d, s).start())

    each(1, n_cols, lambda k: lz_out(k).start())

    for i in range(tiles):
        for p in range(2):
            a, b = split(row_ref[i, p])
            at = pl.ds(p * half + i * ranks, ranks)
            xh[at, :] = a
            xl[at, :] = b

    for copy in own:
        copy.wait()

    near = chips * (nsub - 1)
    total = 2 * (near + chips + nsub - 1)
    spread_at = jnp.where(c == 0, 2, 0)
    final_at = jnp.where(c == 0, total - 1, 2 * (near + chips - 1 - c) + 1)

    def finish():
        def pass_on(d2):
            o = ahead(d2)
            rcopy(lz, lg.at[h, o], lg_send.at[d2], lg_recv.at[h, o], sib).wait_recv()
            lg_forward(d2).start()

        each(1, chips, pass_on)

        each(1, n_cols, lambda k: rcopy(
            eb.at[(c + k) % n_cols], eb.at[(c + k) % n_cols], e_send.at[k], e_recv.at[(c + k) % n_cols], sib
        ).wait_recv())
        entries = jnp.sum(eb[...], axis=0)
        lines = []
        levels = lax.broadcasted_iota(jnp.int32, (1, ranks), 1)
        for i in range(tiles):
            er, ei = entries[2 * i:2 * i + 1], entries[2 * i + 1:2 * i + 2]
            keep = (levels < RANK_STEP * rank_ref[i]).astype(jnp.float32)
            mag = jnp.maximum(er * er + ei * ei, 1.0)
            lines.append(keep * er / mag)
            lines.append(-keep * ei / mag)
        lines.append(jnp.zeros((128 - 2 * tiles, ranks), jnp.float32))
        turned = jnp.concatenate(lines, axis=0).T
        for i in range(tiles):
            fr, fi = turned[:, 2 * i:2 * i + 1], turned[:, 2 * i + 1:2 * i + 2]
            lr, li = i * ranks, half + i * ranks
            vr, vi = [], []
            for hh in range(2):
                for s in range(nsub):
                    vr.append(ps[2 * c + hh, s, lr:lr + ranks, :])
                    vi.append(ps[2 * c + hh, s, li:li + ranks, :])
            vr, vi = jnp.concatenate(vr, axis=1), jnp.concatenate(vi, axis=1)
            wr = vr * fr - vi * fi
            wi = vr * fi + vi * fr
            panel_ref[i, 0] = wr
            panel_ref[i, 1] = wi
            a, b = split(wr)
            ch[lr:lr + ranks, :] = a
            cl[lr:lr + ranks, :] = b
            a, b = split(wi)
            ch[li:li + ranks, :] = a
            cl[li:li + ranks, :] = b

        pltpu.make_async_copy(lz, lg.at[h, q], lg_loc.at[0]).wait()
        each(0, chips, lambda o: rcopy(
            lz, lg.at[1 - h, o], lg_sib.at[0], lg_recv.at[1 - h, o], sib
        ).wait_recv())

        def core(k0, carry):
            k = jnp.where(c == 0, n_cols - 1 - k0, (k0 + 1) % n_cols)
            j = (c + k) % n_cols
            lr = lg[0, :, j].reshape(wc, lz.shape[2])
            li = lg[1, :, j].reshape(wc, lz.shape[2])
            rank2 = lz.shape[2]
            uh, ul = split(jnp.concatenate([lr, li], axis=1))
            prod = dot3(ch[...], cl[...], uh, ul)
            real = prod[:half, :rank2] - prod[half:, rank2:]
            imag = prod[:half, rank2:] + prod[half:, :rank2]
            for i in range(tiles):
                ks[k, i, 0] = real[i * ranks:(i + 1) * ranks]
                ks[k, i, 1] = imag[i * ranks:(i + 1) * ranks]

            @pl.when(k > 0)
            def _():
                k_out(k).start()

            return carry

        lax.fori_loop(0, n_cols, core, 0)

    def share():
        pos = c * wc + lax.broadcasted_iota(jnp.int32, (wc, ranks), 0)
        parts = []
        for i in range(tiles):
            hit = pos == piv_ref[i:i + 1, :]
            for p in range(2):
                parts.append(jnp.sum(jnp.where(hit, col_ref[i, p], 0.0), axis=0, keepdims=True))
        parts.append(jnp.zeros((eb.shape[1] - 2 * tiles, ranks), jnp.float32))
        eb[c] = jnp.concatenate(parts, axis=0)
        each(1, n_cols, lambda k: e_out(k).start())

    def unit(u, carry):
        slot = u // 2
        t = jnp.where(slot < near, ahead(slot % chips), jnp.maximum(near + chips - 1 - slot, 0))
        s = jnp.where(slot < near, slot // chips, jnp.where(slot < near + chips, nsub - 1, slot - near - chips))
        live = jnp.logical_and(t >= c, jnp.logical_or(slot >= near, t > 0))
        e = u % 2
        b = t * 2 + (h + e) % 2

        @pl.when(u == spread_at)
        def _():
            lz_own.wait()
            each(1, n_cols, lambda k: rcopy(
                lz.at[(c + k) % n_cols], lz.at[(c + k) % n_cols], lz_send.at[k], lz_recv.at[(c + k) % n_cols], sib
            ).wait_recv())
            lg_side().start()
            pltpu.make_async_copy(lz, lg.at[h, q], lg_loc.at[0]).start()
            each(1, chips, lambda d2: lg_out(d2).start())
            share()

        @pl.when(live)
        def _():
            @pl.when(jnp.logical_or(t != q, e > 0))
            def _():
                u_forward(t, s, b).wait_recv()

            @pl.when(jnp.logical_and(t != q, e == 0))
            def _():
                u_forward(t, s, b).start()

            ur, ui = us[b, s, 0], us[b, s, 1]
            uh, ul = split(jnp.concatenate([ur, ui], axis=1))
            prod = dot3(xh[...], xl[...], uh, ul)
            fin[0:half] = prod[:half, :sw] - prod[half:, sw:]
            fin[half:2 * half] = prod[:half, sw:] + prod[half:, :sw]

            @pl.when(c > 0)
            def _():
                rcopy(ps.at[b, s], pr.at[b, s], p_send.at[b, s], p_recv.at[b, s], sib).wait_recv()
                ps[b, s] = fin[...] + pr[b, s]

            @pl.when(c == 0)
            def _():
                ps[b, s] = fin[...]

            @pl.when(t > c)
            def _():
                p_up(b, s).start()

        @pl.when(u == final_at)
        def _():
            finish()

        return carry

    lax.fori_loop(0, total, unit, 0)
    cores_ref[:, 0] = ks[0]

    def gather(k):
        o = (c + k) % n_cols
        rcopy(ks.at[k], kr.at[o], k_send.at[k], k_recv.at[o], sib).wait_recv()
        cores_ref[:, 0] = cores_ref[:, 0] + kr[o]

    each(1, n_cols, gather)

    @pl.when(q >= c)
    def _():
        for s in range(nsub):
            u_side(s).wait_send()

        def left(d):
            for s in range(nsub):
                u_out(d, s).wait_send()

        each(1, chips, left)

    def rest(d):
        t = ahead(d)

        @pl.when(jnp.logical_and(t >= c, d > 0))
        def _():
            for s in range(nsub):
                u_forward(t, s, t * 2 + h).wait_send()

        @pl.when(t > c)
        def _():
            for s in range(nsub):
                for e in range(2):
                    p_up(t * 2 + e, s).wait_send()

        @pl.when(d > 0)
        def _():
            lg_out(d).wait_send()
            lg_forward(d).wait_send()

    each(0, chips, rest)
    lg_side().wait_send()

    def tail(k):
        lz_out(k).wait_send()
        k_out(k).wait_send()
        e_out(k).wait_send()

    each(1, n_cols, tail)


def on_device(n_rows, n_cols, col_samples, row_samples, pivot_rows, rank_blocks, upper_inverse, upanel_left):
    tiles, _, ranks, wc = row_samples.shape
    wr = upper_inverse.shape[2]
    left_ranks = upanel_left.shape[3]
    chips = n_rows // 2
    if chips != n_cols or wc != 2 * wr:
        raise ValueError("unsupported mesh")
    nsub = max(wr // 128, 1)
    sw = wr // nsub
    wq = wc // chips
    m = 2 * tiles * ranks
    f32, bf16 = jnp.float32, jnp.bfloat16
    dma = pltpu.SemaphoreType.DMA
    vmem = pl.BlockSpec(memory_space=pltpu.VMEM)
    hbm = pl.BlockSpec(memory_space=pl.ANY)
    return pl.pallas_call(
        functools.partial(kernel, n_rows, n_cols),
        out_shape=(
            jax.ShapeDtypeStruct((tiles, 2, ranks, wc), f32),
            jax.ShapeDtypeStruct((tiles, 1, 2, ranks, left_ranks), f32),
        ),
        in_specs=[vmem, hbm, hbm, vmem, vmem, pl.BlockSpec(memory_space=pltpu.SMEM)],
        out_specs=(vmem, vmem),
        scratch_shapes=[
            pltpu.VMEM((m, wc), bf16),
            pltpu.VMEM((m, wc), bf16),
            pltpu.VMEM((m, wc), bf16),
            pltpu.VMEM((m, wc), bf16),
            pltpu.VMEM((n_rows, nsub, 2, wc, sw), f32),
            pltpu.VMEM((n_rows, nsub, m, sw), f32),
            pltpu.VMEM((n_rows, nsub, m, sw), f32),
            pltpu.VMEM((m, sw), f32),
            pltpu.VMEM((n_cols, wq, left_ranks), f32),
            pltpu.VMEM((2, chips, n_cols, wq, left_ranks), f32),
            pltpu.VMEM((n_cols, tiles, 2, ranks, left_ranks), f32),
            pltpu.VMEM((n_cols, tiles, 2, ranks, left_ranks), f32),
            pltpu.VMEM((n_cols, -(-2 * tiles // 8) * 8, ranks), f32),
            dma((nsub,)), dma((chips, nsub)), dma((nsub,)), dma((chips, nsub)), dma((n_rows, nsub)),
            dma((n_rows, nsub)), dma((n_rows, nsub)),
            dma((1,)), dma((n_cols,)), dma((n_cols,)), dma((1,)), dma((chips,)), dma((1,)), dma((chips,)),
            dma((2, chips)),
            dma((n_cols,)), dma((n_cols,)), dma((n_cols,)), dma((n_cols,)),
        ],
        compiler_params=pltpu.CompilerParams(
            collective_id=0, has_side_effects=True, vmem_limit_bytes=56 * 1024 * 1024
        ),
    )(row_samples, upper_inverse, upanel_left, col_samples, pivot_rows, rank_blocks)


def solution(mesh):
    in_specs = (
        P("row", None, "col", None),
        P("row", None, None, "col"),
        P("row", None),
        P("row"),
        P(None, "col", "row"),
        P("col", None, None, None),
    )
    out_specs = (P("row", None, None, "col"), P("row", "col", None, None, None))
    body = functools.partial(on_device, mesh.shape["row"], mesh.shape["col"])
    return jax.shard_map(body, mesh=mesh, in_specs=in_specs, out_specs=out_specs, check_vma=False)
```

```python
import functools
import math

import jax
import jax.numpy as jnp
from jax import lax
from jax.experimental import pallas as pl
from jax.experimental.pallas import tpu as pltpu
from jax.sharding import PartitionSpec as P

RANK_STEP = 16
MESH = pl.DeviceIdType.MESH


def split(x):
    high = x.astype(jnp.bfloat16)
    low = (x - high.astype(jnp.float32)).astype(jnp.bfloat16)
    return high, low


def dot3(xh, xl, uh, ul):
    def single(a, b):
        return jnp.dot(a, b, preferred_element_type=jnp.float32)

    return single(xh, uh) + (single(xh, ul) + single(xl, uh))


def kernel(
    n_rows, n_cols,
    row_ref, u_ref, up_ref, col_ref, piv_ref, rank_ref,
    panel_ref, cores_ref,
    xh, xl, ch, cl, us, ps, pr, fin, lz, lg, ks, kr, eb,
    u_loc, u_send, u_sib, u_fwd, u_recv,
    p_send, p_recv,
    lz_loc, lz_send, lz_recv, lg_loc, lg_send, lg_sib, lg_fwd, lg_recv,
    k_send, k_recv, e_send, e_recv,
):
    r, c = lax.axis_index("row"), lax.axis_index("col")
    chips = n_rows // 2
    nx = math.isqrt(chips)
    ny = chips // nx
    q, h = r // 2, r % 2
    qy, qx = q // nx, q % nx
    tiles, _, ranks, wc = row_ref.shape
    nsub, sw = us.shape[1], us.shape[4]
    wq = lz.shape[1]
    half = tiles * ranks
    sib = (q * 2 + 1 - h, c)

    def ahead(d):
        return ((qy + d // nx) % ny) * nx + (qx + d % nx) % nx

    def behind(d):
        return ((qy + ny - d // nx) % ny) * nx + (qx + nx - d % nx) % nx

    def rcopy(src, dst, ssem, rsem, dev):
        return pltpu.make_async_remote_copy(
            src_ref=src, dst_ref=dst, send_sem=ssem, recv_sem=rsem, device_id=dev, device_id_type=MESH
        )

    def u_out(d, s):
        return rcopy(
            u_ref.at[:, :, s * sw:(s + 1) * sw], us.at[r, s], u_send.at[d, s], u_recv.at[r, s],
            (behind(d) * 2 + h, c),
        )

    def u_side(s):
        return rcopy(u_ref.at[:, :, s * sw:(s + 1) * sw], us.at[r, s], u_sib.at[s], u_recv.at[r, s], sib)

    def u_forward(t, s, b):
        return rcopy(us.at[b, s], us.at[b, s], u_fwd.at[t, s], u_recv.at[b, s], sib)

    square = nx == 2 and ny == 2
    direct = chips - 1 if square else chips

    def u_relay(s, b):
        to = behind(1) if s % 2 == 0 else behind(2)
        return rcopy(us.at[b, s], us.at[b, s], u_send.at[chips - 1, s], u_recv.at[b, s], (to * 2 + h, c))

    def p_up(b, s):
        return rcopy(ps.at[b, s], pr.at[b, s], p_send.at[b, s], p_recv.at[b, s], (r, c + 1))

    def lz_out(k):
        to = (c + k) % n_cols
        start = pl.multiple_of(to * wc + q * wq, wq)
        return rcopy(up_ref.at[0, h, pl.ds(start, wq), :], lz.at[c], lz_send.at[k], lz_recv.at[c], (r, to))

    def lg_out(d):
        return rcopy(lz, lg.at[h, q], lg_send.at[d], lg_recv.at[h, q], (behind(d) * 2 + h, c))

    def lg_side():
        return rcopy(lz, lg.at[h, q], lg_sib.at[0], lg_recv.at[h, q], sib)

    def lg_forward(d):
        b = ahead(d)
        return rcopy(lg.at[h, b], lg.at[h, b], lg_fwd.at[d], lg_recv.at[h, b], sib)

    def k_out(k):
        to = (c + k) % n_cols
        return rcopy(ks.at[k], kr.at[c], k_send.at[k], k_recv.at[c], (r, to))

    def e_out(k):
        return rcopy(eb.at[c], eb.at[c], e_send.at[k], e_recv.at[c], (r, (c + k) % n_cols))

    def each(first, last, body):
        lax.fori_loop(first, last, lambda i, z: (body(i), z)[1], 0)

    own = [
        pltpu.make_async_copy(u_ref.at[:, :, s * sw:(s + 1) * sw], us.at[r, s], u_loc.at[s]) for s in range(nsub)
    ]
    for copy in own:
        copy.start()
    mine = pl.multiple_of(c * wc + q * wq, wq)
    lz_own = pltpu.make_async_copy(up_ref.at[0, h, pl.ds(mine, wq), :], lz.at[c], lz_loc.at[0])
    lz_own.start()
    barrier = pltpu.get_barrier_semaphore()

    def signal(dev):
        pl.semaphore_signal(barrier, inc=1, device_id=dev, device_id_type=MESH)

    signal(sib)
    each(1, chips, lambda d: signal((behind(d) * 2 + h, c)))
    each(1, n_cols, lambda k: signal((r, (c + k) % n_cols)))
    pl.semaphore_wait(barrier, 1 + (chips - 1) + (n_cols - 1))

    @pl.when(q >= c)
    def _():
        for s in range(nsub):
            u_side(s).start()

        for s in range(nsub):
            each(1, direct, lambda d: u_out(d, s).start())

    each(1, n_cols, lambda k: lz_out(k).start())

    for i in range(tiles):
        for p in range(2):
            a, b = split(row_ref[i, p])
            at = pl.ds(p * half + i * ranks, ranks)
            xh[at, :] = a
            xl[at, :] = b

    pos = c * wc + lax.broadcasted_iota(jnp.int32, (wc, ranks), 0)
    parts = []
    for i in range(tiles):
        hit = pos == piv_ref[i:i + 1, :]
        for p in range(2):
            parts.append(jnp.sum(jnp.where(hit, col_ref[i, p], 0.0), axis=0, keepdims=True))
    parts.append(jnp.zeros((eb.shape[1] - 2 * tiles, ranks), jnp.float32))
    eb[c] = jnp.concatenate(parts, axis=0)
    each(1, n_cols, lambda k: e_out(k).start())
    for copy in own:
        copy.wait()

    near = chips * (nsub - 1)
    total = 2 * (near + chips + nsub - 1)
    spread_at = jnp.where(c == 0, 2, 0)
    final_at = jnp.where(c == 0, total - 1, 2 * (near + chips - 1 - c) + 1)

    def finish():
        def pass_on(d2):
            o = ahead(d2)
            rcopy(lz, lg.at[h, o], lg_send.at[d2], lg_recv.at[h, o], sib).wait_recv()
            lg_forward(d2).start()

        each(1, chips, pass_on)

        each(1, n_cols, lambda k: rcopy(
            eb.at[(c + k) % n_cols], eb.at[(c + k) % n_cols], e_send.at[k], e_recv.at[(c + k) % n_cols], sib
        ).wait_recv())
        entries = jnp.sum(eb[...], axis=0)
        lines = []
        levels = lax.broadcasted_iota(jnp.int32, (1, ranks), 1)
        for i in range(tiles):
            er, ei = entries[2 * i:2 * i + 1], entries[2 * i + 1:2 * i + 2]
            keep = (levels < RANK_STEP * rank_ref[i]).astype(jnp.float32)
            mag = jnp.maximum(er * er + ei * ei, 1.0)
            lines.append(keep * er / mag)
            lines.append(-keep * ei / mag)
        lines.append(jnp.zeros((128 - 2 * tiles, ranks), jnp.float32))
        turned = jnp.concatenate(lines, axis=0).T
        for i in range(tiles):
            fr, fi = turned[:, 2 * i:2 * i + 1], turned[:, 2 * i + 1:2 * i + 2]
            lr, li = i * ranks, half + i * ranks
            vr, vi = [], []
            for hh in range(2):
                for s in range(nsub):
                    vr.append(ps[2 * c + hh, s, lr:lr + ranks, :])
                    vi.append(ps[2 * c + hh, s, li:li + ranks, :])
            vr, vi = jnp.concatenate(vr, axis=1), jnp.concatenate(vi, axis=1)
            wr = vr * fr - vi * fi
            wi = vr * fi + vi * fr
            panel_ref[i, 0] = wr
            panel_ref[i, 1] = wi
            a, b = split(wr)
            ch[lr:lr + ranks, :] = a
            cl[lr:lr + ranks, :] = b
            a, b = split(wi)
            ch[li:li + ranks, :] = a
            cl[li:li + ranks, :] = b

        pltpu.make_async_copy(lz, lg.at[h, q], lg_loc.at[0]).wait()
        each(0, chips, lambda o: rcopy(
            lz, lg.at[1 - h, o], lg_sib.at[0], lg_recv.at[1 - h, o], sib
        ).wait_recv())

        def core(k0, carry):
            k = (k0 + 1) % n_cols
            j = (c + k) % n_cols
            lr = lg[0, :, j].reshape(wc, lz.shape[2])
            li = lg[1, :, j].reshape(wc, lz.shape[2])
            rank2 = lz.shape[2]
            uh, ul = split(jnp.concatenate([lr, li], axis=1))
            prod = dot3(ch[...], cl[...], uh, ul)
            real = prod[:half, :rank2] - prod[half:, rank2:]
            imag = prod[:half, rank2:] + prod[half:, :rank2]
            for i in range(tiles):
                ks[k, i, 0] = real[i * ranks:(i + 1) * ranks]
                ks[k, i, 1] = imag[i * ranks:(i + 1) * ranks]

            @pl.when(k > 0)
            def _():
                k_out(k).start()

            return carry

        lax.fori_loop(0, n_cols, core, 0)

    def unit(u, carry):
        slot = u // 2
        t = jnp.where(slot < near, ahead(slot % chips), jnp.maximum(near + chips - 1 - slot, 0))
        s = jnp.where(slot < near, slot // chips, jnp.where(slot < near + chips, nsub - 1, slot - near - chips))
        live = jnp.logical_and(t >= c, jnp.logical_or(slot >= near, t > 0))
        e = u % 2
        b = t * 2 + (h + e) % 2

        @pl.when(u == spread_at)
        def _():
            lz_own.wait()
            each(1, n_cols, lambda k: rcopy(
                lz.at[(c + k) % n_cols], lz.at[(c + k) % n_cols], lz_send.at[k], lz_recv.at[(c + k) % n_cols], sib
            ).wait_recv())
            lg_side().start()
            pltpu.make_async_copy(lz, lg.at[h, q], lg_loc.at[0]).start()
            each(1, chips, lambda d2: lg_out(d2).start())

        @pl.when(live)
        def _():
            @pl.when(jnp.logical_or(t != q, e > 0))
            def _():
                u_forward(t, s, b).wait_recv()

            @pl.when(jnp.logical_and(t != q, e == 0))
            def _():
                u_forward(t, s, b).start()

            if square:
                for s2 in range(nsub):
                    source = ahead(2 - s2 % 2)

                    @pl.when(jnp.logical_and(e == 0, jnp.logical_and(s == s2, t == source)))
                    def _():
                        u_relay(s2, source * 2 + h).start()

            ur, ui = us[b, s, 0], us[b, s, 1]
            uh, ul = split(jnp.concatenate([ur, ui], axis=1))
            prod = dot3(xh[...], xl[...], uh, ul)
            fin[0:half] = prod[:half, :sw] - prod[half:, sw:]
            fin[half:2 * half] = prod[:half, sw:] + prod[half:, :sw]

            @pl.when(c > 0)
            def _():
                rcopy(ps.at[b, s], pr.at[b, s], p_send.at[b, s], p_recv.at[b, s], sib).wait_recv()
                ps[b, s] = fin[...] + pr[b, s]

            @pl.when(c == 0)
            def _():
                ps[b, s] = fin[...]

            @pl.when(t > c)
            def _():
                p_up(b, s).start()

        @pl.when(u == final_at)
        def _():
            finish()

        return carry

    lax.fori_loop(0, total, unit, 0)
    cores_ref[:, 0] = ks[0]

    def gather(k):
        o = (c + k) % n_cols
        rcopy(ks.at[k], kr.at[o], k_send.at[k], k_recv.at[o], sib).wait_recv()
        cores_ref[:, 0] = cores_ref[:, 0] + kr[o]

    each(1, n_cols, gather)

    @pl.when(q >= c)
    def _():
        for s in range(nsub):
            u_side(s).wait_send()

        def left(d):
            for s in range(nsub):
                u_out(d, s).wait_send()

        each(1, direct, left)

    if square:
        for s in range(nsub):
            source = ahead(2 - s % 2)

            @pl.when(source >= c)
            def _():
                u_relay(s, source * 2 + h).wait_send()

    def rest(d):
        t = ahead(d)

        @pl.when(jnp.logical_and(t >= c, d > 0))
        def _():
            for s in range(nsub):
                u_forward(t, s, t * 2 + h).wait_send()

        @pl.when(t > c)
        def _():
            for s in range(nsub):
                for e in range(2):
                    p_up(t * 2 + e, s).wait_send()

        @pl.when(d > 0)
        def _():
            lg_out(d).wait_send()
            lg_forward(d).wait_send()

    each(0, chips, rest)
    lg_side().wait_send()

    def tail(k):
        lz_out(k).wait_send()
        k_out(k).wait_send()
        e_out(k).wait_send()

    each(1, n_cols, tail)


def on_device(n_rows, n_cols, col_samples, row_samples, pivot_rows, rank_blocks, upper_inverse, upanel_left):
    tiles, _, ranks, wc = row_samples.shape
    wr = upper_inverse.shape[2]
    left_ranks = upanel_left.shape[3]
    chips = n_rows // 2
    if chips != n_cols or wc != 2 * wr:
        raise ValueError("unsupported mesh")
    nsub = max(wr // 128, 1)
    sw = wr // nsub
    wq = wc // chips
    m = 2 * tiles * ranks
    f32, bf16 = jnp.float32, jnp.bfloat16
    dma = pltpu.SemaphoreType.DMA
    vmem = pl.BlockSpec(memory_space=pltpu.VMEM)
    hbm = pl.BlockSpec(memory_space=pl.ANY)
    return pl.pallas_call(
        functools.partial(kernel, n_rows, n_cols),
        out_shape=(
            jax.ShapeDtypeStruct((tiles, 2, ranks, wc), f32),
            jax.ShapeDtypeStruct((tiles, 1, 2, ranks, left_ranks), f32),
        ),
        in_specs=[vmem, hbm, hbm, vmem, vmem, pl.BlockSpec(memory_space=pltpu.SMEM)],
        out_specs=(vmem, vmem),
        scratch_shapes=[
            pltpu.VMEM((m, wc), bf16),
            pltpu.VMEM((m, wc), bf16),
            pltpu.VMEM((m, wc), bf16),
            pltpu.VMEM((m, wc), bf16),
            pltpu.VMEM((n_rows, nsub, 2, wc, sw), f32),
            pltpu.VMEM((n_rows, nsub, m, sw), f32),
            pltpu.VMEM((n_rows, nsub, m, sw), f32),
            pltpu.VMEM((m, sw), f32),
            pltpu.VMEM((n_cols, wq, left_ranks), f32),
            pltpu.VMEM((2, chips, n_cols, wq, left_ranks), f32),
            pltpu.VMEM((n_cols, tiles, 2, ranks, left_ranks), f32),
            pltpu.VMEM((n_cols, tiles, 2, ranks, left_ranks), f32),
            pltpu.VMEM((n_cols, -(-2 * tiles // 8) * 8, ranks), f32),
            dma((nsub,)), dma((chips, nsub)), dma((nsub,)), dma((chips, nsub)), dma((n_rows, nsub)),
            dma((n_rows, nsub)), dma((n_rows, nsub)),
            dma((1,)), dma((n_cols,)), dma((n_cols,)), dma((1,)), dma((chips,)), dma((1,)), dma((chips,)),
            dma((2, chips)),
            dma((n_cols,)), dma((n_cols,)), dma((n_cols,)), dma((n_cols,)),
        ],
        compiler_params=pltpu.CompilerParams(
            collective_id=0, has_side_effects=True, vmem_limit_bytes=56 * 1024 * 1024
        ),
    )(row_samples, upper_inverse, upanel_left, col_samples, pivot_rows, rank_blocks)


def solution(mesh):
    in_specs = (
        P("row", None, "col", None),
        P("row", None, None, "col"),
        P("row", None),
        P("row"),
        P(None, "col", "row"),
        P("col", None, None, None),
    )
    out_specs = (P("row", None, None, "col"), P("row", "col", None, None, None))
    body = functools.partial(on_device, mesh.shape["row"], mesh.shape["col"])
    return jax.shard_map(body, mesh=mesh, in_specs=in_specs, out_specs=out_specs, check_vma=False)
```

```python
import functools
import math

import jax
import jax.numpy as jnp
from jax import lax
from jax.experimental import pallas as pl
from jax.experimental.pallas import tpu as pltpu
from jax.sharding import PartitionSpec as P

RANK_STEP = 16
MESH = pl.DeviceIdType.MESH


def split(x):
    high = x.astype(jnp.bfloat16)
    low = (x - high.astype(jnp.float32)).astype(jnp.bfloat16)
    return high, low


def dot3(xh, xl, uh, ul):
    def single(a, b):
        return jnp.dot(a, b, preferred_element_type=jnp.float32)

    return single(xh, uh) + (single(xh, ul) + single(xl, uh))


def kernel(
    n_rows, n_cols,
    row_ref, u_ref, up_ref, col_ref, piv_ref, rank_ref,
    panel_ref, cores_ref,
    xh, xl, ch, cl, us, ps, pr, fin, lz, lg, ks, kr, eb,
    u_loc, u_send, u_sib, u_fwd, u_recv,
    p_send, p_recv,
    lz_loc, lz_send, lz_recv, lg_loc, lg_send, lg_sib, lg_fwd, lg_recv,
    k_send, k_recv, e_send, e_recv,
):
    r, c = lax.axis_index("row"), lax.axis_index("col")
    chips = n_rows // 2
    nx = math.isqrt(chips)
    ny = chips // nx
    q, h = r // 2, r % 2
    qy, qx = q // nx, q % nx
    tiles, _, ranks, wc = row_ref.shape
    nsub, sw = us.shape[1], us.shape[4]
    wq = lz.shape[1]
    half = tiles * ranks
    sib = (q * 2 + 1 - h, c)

    def ahead(d):
        return ((qy + d // nx) % ny) * nx + (qx + d % nx) % nx

    def behind(d):
        return ((qy + ny - d // nx) % ny) * nx + (qx + nx - d % nx) % nx

    def rcopy(src, dst, ssem, rsem, dev):
        return pltpu.make_async_remote_copy(
            src_ref=src, dst_ref=dst, send_sem=ssem, recv_sem=rsem, device_id=dev, device_id_type=MESH
        )

    def u_out(d, s):
        return rcopy(
            u_ref.at[:, :, s * sw:(s + 1) * sw], us.at[r, s], u_send.at[d, s], u_recv.at[r, s],
            (behind(d) * 2 + h, c),
        )

    def u_side(s):
        return rcopy(u_ref.at[:, :, s * sw:(s + 1) * sw], us.at[r, s], u_sib.at[s], u_recv.at[r, s], sib)

    def u_forward(t, s, b):
        return rcopy(us.at[b, s], us.at[b, s], u_fwd.at[t, s], u_recv.at[b, s], sib)

    def p_up(b, s):
        return rcopy(ps.at[b, s], pr.at[b, s], p_send.at[b, s], p_recv.at[b, s], (r, c + 1))

    def lz_out(k):
        to = (c + k) % n_cols
        start = pl.multiple_of(to * wc + q * wq, wq)
        return rcopy(up_ref.at[0, h, pl.ds(start, wq), :], lz.at[c], lz_send.at[k], lz_recv.at[c], (r, to))

    def lg_out(d):
        return rcopy(lz, lg.at[h, q], lg_send.at[d], lg_recv.at[h, q], (behind(d) * 2 + h, c))

    def lg_side():
        return rcopy(lz, lg.at[h, q], lg_sib.at[0], lg_recv.at[h, q], sib)

    def lg_forward(d):
        b = ahead(d)
        return rcopy(lg.at[h, b], lg.at[h, b], lg_fwd.at[d], lg_recv.at[h, b], sib)

    def k_out(k):
        to = (c + k) % n_cols
        return rcopy(ks.at[k], kr.at[c], k_send.at[k], k_recv.at[c], (r, to))

    def e_out(k):
        return rcopy(eb.at[c], eb.at[c], e_send.at[k], e_recv.at[c], (r, (c + k) % n_cols))

    def each(first, last, body):
        lax.fori_loop(first, last, lambda i, z: (body(i), z)[1], 0)

    own = [
        pltpu.make_async_copy(u_ref.at[:, :, s * sw:(s + 1) * sw], us.at[r, s], u_loc.at[s]) for s in range(nsub)
    ]
    for copy in own:
        copy.start()
    mine = pl.multiple_of(c * wc + q * wq, wq)
    lz_own = pltpu.make_async_copy(up_ref.at[0, h, pl.ds(mine, wq), :], lz.at[c], lz_loc.at[0])
    lz_own.start()
    barrier = pltpu.get_barrier_semaphore()

    def signal(dev):
        pl.semaphore_signal(barrier, inc=1, device_id=dev, device_id_type=MESH)

    signal(sib)
    each(1, chips, lambda d: signal((behind(d) * 2 + h, c)))
    each(1, n_cols, lambda k: signal((r, (c + k) % n_cols)))
    pl.semaphore_wait(barrier, 1 + (chips - 1) + (n_cols - 1))

    @pl.when(q >= c)
    def _():
        for s in range(nsub):
            u_side(s).start()

        @pl.when(q > 0)
        def _():
            for s in range(nsub):
                each(1, chips, lambda d: u_out(d, s).start())

    each(1, n_cols, lambda k: lz_out(k).start())

    for i in range(tiles):
        for p in range(2):
            a, b = split(row_ref[i, p])
            at = pl.ds(p * half + i * ranks, ranks)
            xh[at, :] = a
            xl[at, :] = b

    pos = c * wc + lax.broadcasted_iota(jnp.int32, (wc, ranks), 0)
    parts = []
    for i in range(tiles):
        hit = pos == piv_ref[i:i + 1, :]
        for p in range(2):
            parts.append(jnp.sum(jnp.where(hit, col_ref[i, p], 0.0), axis=0, keepdims=True))
    parts.append(jnp.zeros((eb.shape[1] - 2 * tiles, ranks), jnp.float32))
    eb[c] = jnp.concatenate(parts, axis=0)
    each(1, n_cols, lambda k: e_out(k).start())
    for copy in own:
        copy.wait()

    near = chips * (nsub - 1)
    total = 2 * (near + chips + nsub - 1)
    spread_at = jnp.where(c == 0, 2, 0)
    final_at = jnp.where(c == 0, total - 1, 2 * (near + chips - 1 - c) + 1)

    def finish():
        def pass_on(d2):
            o = ahead(d2)
            rcopy(lz, lg.at[h, o], lg_send.at[d2], lg_recv.at[h, o], sib).wait_recv()
            lg_forward(d2).start()

        each(1, chips, pass_on)

        each(1, n_cols, lambda k: rcopy(
            eb.at[(c + k) % n_cols], eb.at[(c + k) % n_cols], e_send.at[k], e_recv.at[(c + k) % n_cols], sib
        ).wait_recv())
        entries = jnp.sum(eb[...], axis=0)
        lines = []
        levels = lax.broadcasted_iota(jnp.int32, (1, ranks), 1)
        for i in range(tiles):
            er, ei = entries[2 * i:2 * i + 1], entries[2 * i + 1:2 * i + 2]
            keep = (levels < RANK_STEP * rank_ref[i]).astype(jnp.float32)
            mag = jnp.maximum(er * er + ei * ei, 1.0)
            lines.append(keep * er / mag)
            lines.append(-keep * ei / mag)
        lines.append(jnp.zeros((128 - 2 * tiles, ranks), jnp.float32))
        turned = jnp.concatenate(lines, axis=0).T
        for i in range(tiles):
            fr, fi = turned[:, 2 * i:2 * i + 1], turned[:, 2 * i + 1:2 * i + 2]
            lr, li = i * ranks, half + i * ranks
            vr, vi = [], []
            for hh in range(2):
                for s in range(nsub):
                    vr.append(ps[2 * c + hh, s, lr:lr + ranks, :])
                    vi.append(ps[2 * c + hh, s, li:li + ranks, :])
            vr, vi = jnp.concatenate(vr, axis=1), jnp.concatenate(vi, axis=1)
            wr = vr * fr - vi * fi
            wi = vr * fi + vi * fr
            panel_ref[i, 0] = wr
            panel_ref[i, 1] = wi
            a, b = split(wr)
            ch[lr:lr + ranks, :] = a
            cl[lr:lr + ranks, :] = b
            a, b = split(wi)
            ch[li:li + ranks, :] = a
            cl[li:li + ranks, :] = b

        pltpu.make_async_copy(lz, lg.at[h, q], lg_loc.at[0]).wait()
        each(0, chips, lambda o: rcopy(
            lz, lg.at[1 - h, o], lg_sib.at[0], lg_recv.at[1 - h, o], sib
        ).wait_recv())

        def core(k0, carry):
            k = jnp.where(c == 0, n_cols - 1 - k0, (k0 + 1) % n_cols)
            j = (c + k) % n_cols
            lr = lg[0, :, j].reshape(wc, lz.shape[2])
            li = lg[1, :, j].reshape(wc, lz.shape[2])
            rank2 = lz.shape[2]
            uh, ul = split(jnp.concatenate([lr, li], axis=1))
            prod = dot3(ch[...], cl[...], uh, ul)
            real = prod[:half, :rank2] - prod[half:, rank2:]
            imag = prod[:half, rank2:] + prod[half:, :rank2]
            for i in range(tiles):
                ks[k, i, 0] = real[i * ranks:(i + 1) * ranks]
                ks[k, i, 1] = imag[i * ranks:(i + 1) * ranks]

            @pl.when(k > 0)
            def _():
                k_out(k).start()

            return carry

        lax.fori_loop(0, n_cols, core, 0)

    def unit(u, carry):
        slot = u // 2
        t = jnp.where(slot < near, ahead(slot % chips), jnp.maximum(near + chips - 1 - slot, 0))
        s = jnp.where(slot < near, slot // chips, jnp.where(slot < near + chips, nsub - 1, slot - near - chips))
        live = jnp.logical_and(t >= c, jnp.logical_or(slot >= near, t > 0))
        e = u % 2
        b = t * 2 + (h + e) % 2

        @pl.when(u == spread_at)
        def _():
            lz_own.wait()
            each(1, n_cols, lambda k: rcopy(
                lz.at[(c + k) % n_cols], lz.at[(c + k) % n_cols], lz_send.at[k], lz_recv.at[(c + k) % n_cols], sib
            ).wait_recv())
            lg_side().start()
            pltpu.make_async_copy(lz, lg.at[h, q], lg_loc.at[0]).start()
            each(1, chips, lambda d2: lg_out(d2).start())

            @pl.when(jnp.logical_and(q == 0, q >= c))
            def _():
                for s2 in range(nsub):
                    each(1, chips, lambda d2: u_out(d2, s2).start())

        @pl.when(live)
        def _():
            @pl.when(jnp.logical_or(t != q, e > 0))
            def _():
                u_forward(t, s, b).wait_recv()

            @pl.when(jnp.logical_and(t != q, e == 0))
            def _():
                u_forward(t, s, b).start()

            ur, ui = us[b, s, 0], us[b, s, 1]
            uh, ul = split(jnp.concatenate([ur, ui], axis=1))
            prod = dot3(xh[...], xl[...], uh, ul)
            fin[0:half] = prod[:half, :sw] - prod[half:, sw:]
            fin[half:2 * half] = prod[:half, sw:] + prod[half:, :sw]

            @pl.when(c > 0)
            def _():
                rcopy(ps.at[b, s], pr.at[b, s], p_send.at[b, s], p_recv.at[b, s], sib).wait_recv()
                ps[b, s] = fin[...] + pr[b, s]

            @pl.when(c == 0)
            def _():
                ps[b, s] = fin[...]

            @pl.when(t > c)
            def _():
                p_up(b, s).start()

        @pl.when(u == final_at)
        def _():
            finish()

        return carry

    lax.fori_loop(0, total, unit, 0)
    cores_ref[:, 0] = ks[0]

    def gather(k):
        o = (c + k) % n_cols
        rcopy(ks.at[k], kr.at[o], k_send.at[k], k_recv.at[o], sib).wait_recv()
        cores_ref[:, 0] = cores_ref[:, 0] + kr[o]

    each(1, n_cols, gather)

    @pl.when(q >= c)
    def _():
        for s in range(nsub):
            u_side(s).wait_send()

        def left(d):
            for s in range(nsub):
                u_out(d, s).wait_send()

        each(1, chips, left)

    def rest(d):
        t = ahead(d)

        @pl.when(jnp.logical_and(t >= c, d > 0))
        def _():
            for s in range(nsub):
                u_forward(t, s, t * 2 + h).wait_send()

        @pl.when(t > c)
        def _():
            for s in range(nsub):
                for e in range(2):
                    p_up(t * 2 + e, s).wait_send()

        @pl.when(d > 0)
        def _():
            lg_out(d).wait_send()
            lg_forward(d).wait_send()

    each(0, chips, rest)
    lg_side().wait_send()

    def tail(k):
        lz_out(k).wait_send()
        k_out(k).wait_send()
        e_out(k).wait_send()

    each(1, n_cols, tail)


def on_device(n_rows, n_cols, col_samples, row_samples, pivot_rows, rank_blocks, upper_inverse, upanel_left):
    tiles, _, ranks, wc = row_samples.shape
    wr = upper_inverse.shape[2]
    left_ranks = upanel_left.shape[3]
    chips = n_rows // 2
    if chips != n_cols or wc != 2 * wr:
        raise ValueError("unsupported mesh")
    nsub = max(wr // 128, 1)
    sw = wr // nsub
    wq = wc // chips
    m = 2 * tiles * ranks
    f32, bf16 = jnp.float32, jnp.bfloat16
    dma = pltpu.SemaphoreType.DMA
    vmem = pl.BlockSpec(memory_space=pltpu.VMEM)
    hbm = pl.BlockSpec(memory_space=pl.ANY)
    return pl.pallas_call(
        functools.partial(kernel, n_rows, n_cols),
        out_shape=(
            jax.ShapeDtypeStruct((tiles, 2, ranks, wc), f32),
            jax.ShapeDtypeStruct((tiles, 1, 2, ranks, left_ranks), f32),
        ),
        in_specs=[vmem, hbm, hbm, vmem, vmem, pl.BlockSpec(memory_space=pltpu.SMEM)],
        out_specs=(vmem, vmem),
        scratch_shapes=[
            pltpu.VMEM((m, wc), bf16),
            pltpu.VMEM((m, wc), bf16),
            pltpu.VMEM((m, wc), bf16),
            pltpu.VMEM((m, wc), bf16),
            pltpu.VMEM((n_rows, nsub, 2, wc, sw), f32),
            pltpu.VMEM((n_rows, nsub, m, sw), f32),
            pltpu.VMEM((n_rows, nsub, m, sw), f32),
            pltpu.VMEM((m, sw), f32),
            pltpu.VMEM((n_cols, wq, left_ranks), f32),
            pltpu.VMEM((2, chips, n_cols, wq, left_ranks), f32),
            pltpu.VMEM((n_cols, tiles, 2, ranks, left_ranks), f32),
            pltpu.VMEM((n_cols, tiles, 2, ranks, left_ranks), f32),
            pltpu.VMEM((n_cols, -(-2 * tiles // 8) * 8, ranks), f32),
            dma((nsub,)), dma((chips, nsub)), dma((nsub,)), dma((chips, nsub)), dma((n_rows, nsub)),
            dma((n_rows, nsub)), dma((n_rows, nsub)),
            dma((1,)), dma((n_cols,)), dma((n_cols,)), dma((1,)), dma((chips,)), dma((1,)), dma((chips,)),
            dma((2, chips)),
            dma((n_cols,)), dma((n_cols,)), dma((n_cols,)), dma((n_cols,)),
        ],
        compiler_params=pltpu.CompilerParams(
            collective_id=0, has_side_effects=True, vmem_limit_bytes=56 * 1024 * 1024
        ),
    )(row_samples, upper_inverse, upanel_left, col_samples, pivot_rows, rank_blocks)


def solution(mesh):
    in_specs = (
        P("row", None, "col", None),
        P("row", None, None, "col"),
        P("row", None),
        P("row"),
        P(None, "col", "row"),
        P("col", None, None, None),
    )
    out_specs = (P("row", None, None, "col"), P("row", "col", None, None, None))
    body = functools.partial(on_device, mesh.shape["row"], mesh.shape["col"])
    return jax.shard_map(body, mesh=mesh, in_specs=in_specs, out_specs=out_specs, check_vma=False)
```
